32 devices in a mesh: gx: 2 (over core), gy: 4 (over z), gz: 4 (over y, x).
Axes of the slice: x: 2, y: 2, z: 4, core: 2. Of those that a mesh axis runs over, the one named last changes fastest.
Arguments:
- density_volume: float32 [64, 512, 512], P('gz', 'gy', 'gx'), may hold values from -4 to 4
Outputs:
- colour: float32 [3, 512, 512], P(None, ('gy', 'gz'), 'gx')
- depth_map: float32 [512, 512], P(('gy', 'gz'), 'gx')
- transparency: float32 [512, 512], P(('gy', 'gz'), 'gx')
The draws below stay inside these ranges and needn't reach their ends.
All inputs are finite; a program needn't handle non-finite values.
Results may differ from the reference program's by a relative error of at most 0.0003.
Values sent between devices are 32-bit elements; how exact they have to be, the bound alone decides.
No kernel may reach another device: no remote copies, remote signals or barrier semaphores. Data moves between devices by JAX's collectives and lax.ppermute only.
A program may use at most 128 MiB of HBM per device.

```python
import jax
import jax.numpy as jnp
from jax import lax

NX = 512
NY = 512
NZ = 64


def steps_of(stream_key, dims, cuts, least, top_value):
    gain = 1.0
    for axis_at, parts in cuts:
        draws = jax.random.uniform(jax.random.fold_in(jax.random.fold_in(stream_key, 6), axis_at), (parts,), jnp.float32, least / len(cuts), top_value / len(cuts))
        gain = gain * jnp.repeat(jnp.exp(draws), dims[axis_at] // parts).reshape((-1,) + (1,) * (len(dims) - 1 - axis_at))
    return gain


def bell_draw(stream_key, dims, width, most, cuts=(), held_as=jnp.bfloat16):
    level = steps_of(stream_key, dims, cuts, -0.22, 0.18) if cuts else 1.0
    values = jax.random.normal(stream_key, dims, jnp.float32) * width * level
    return jnp.minimum(jnp.maximum(values, -most), most).astype(held_as)


def setup_inputs(seed: int = 0) -> dict:
    seeds = jax.random.split(jax.random.key(seed), 2)
    density_volume = bell_draw(seeds[0], (NZ, NY, NX), 1.0, 4.0, ((0, 4), (1, 4), (2, 2)), jnp.float32)
    return dict(density_volume=density_volume)


def fourth(far_low, near_low, near_high, far_high):
    return (far_low - 8.0 * near_low + 8.0 * near_high - far_high) / 12.0

def shade(sample, grad_z, grad_y, grad_x):
    square = grad_z * grad_z + grad_y * grad_y + grad_x * grad_x
    facing = (0.64 * grad_z + 0.6 * grad_y + 0.48 * grad_x) * lax.rsqrt(square + 1.0)
    diffuse = 0.3 + 0.7 * jnp.maximum(facing, 0.0)
    edge_gain = 1.0 + square / (square + 1.0)
    density = jax.nn.softplus(sample) * edge_gain
    colour_red = jax.nn.sigmoid(2.0 * sample) * diffuse
    colour_green = jnp.exp(-0.5 * sample * sample) * diffuse
    colour_blue = jax.nn.sigmoid(-2.0 * sample) * diffuse
    return (density, colour_red, colour_green, colour_blue)

def reference(density_volume):
    block_rows = 16
    blocks = NY // block_rows
    depth_step = 2.0 / NZ
    depth_pos = (jnp.arange(NZ, dtype=jnp.int32).astype(jnp.float32) + 0.5) / NZ

    def shade_block(block_index):
        row_index = block_index * block_rows - 2 + jnp.arange(block_rows + 4, dtype=jnp.int32)
        inside = ((row_index >= 0) & (row_index < NY)).astype(jnp.float32)
        slab_rows = jnp.take(density_volume, jnp.clip(row_index, 0, NY - 1).astype(jnp.int32), axis=1)
        slab_rows = slab_rows * inside[None, :, None]
        slab_rows = jnp.pad(slab_rows, ((2, 2), (0, 0), (2, 2)))
        centre = slab_rows[2:-2, 2:-2, 2:-2]
        grad_z = fourth(slab_rows[0:-4, 2:-2, 2:-2], slab_rows[1:-3, 2:-2, 2:-2], slab_rows[3:-1, 2:-2, 2:-2], slab_rows[4:, 2:-2, 2:-2])
        grad_y = fourth(slab_rows[2:-2, 0:-4, 2:-2], slab_rows[2:-2, 1:-3, 2:-2], slab_rows[2:-2, 3:-1, 2:-2], slab_rows[2:-2, 4:, 2:-2])
        grad_x = fourth(slab_rows[2:-2, 2:-2, 0:-4], slab_rows[2:-2, 2:-2, 1:-3], slab_rows[2:-2, 2:-2, 3:-1], slab_rows[2:-2, 2:-2, 4:])
        density, colour_red, colour_green, colour_blue = shade(centre, grad_z, grad_y, grad_x)
        optical = density * depth_step
        inclusive = jnp.cumsum(optical, axis=0)
        weight = jnp.exp(-(inclusive - optical)) * (1.0 - jnp.exp(-optical))
        shaded = jnp.stack([lax.optimization_barrier(jnp.sum(weight * colour_red, axis=0)), lax.optimization_barrier(jnp.sum(weight * colour_green, axis=0)), lax.optimization_barrier(jnp.sum(weight * colour_blue, axis=0))])
        depth_map = lax.optimization_barrier(jnp.sum(weight * depth_pos[:, None, None], axis=0))
        transparency = jnp.exp(-inclusive[-1])
        return (shaded, depth_map, transparency)
    shaded, depth_map, transparency = lax.map(shade_block, jnp.arange(blocks, dtype=jnp.int32))
    colour = jnp.transpose(shaded, (1, 0, 2, 3)).reshape(3, NY, NX)
    return (colour, depth_map.reshape(NY, NX), transparency.reshape(NY, NX))
```

```python
import functools

import jax
import jax.numpy as jnp
from jax import lax
from jax.experimental import pallas as pl
from jax.experimental.pallas import tpu as pltpu
from jax.sharding import PartitionSpec as P

EDGE = 8


def band(offset):
    one = jnp.where(offset == 1, 8.0, jnp.where(offset == -1, -8.0, 0.0))
    two = jnp.where(offset == 2, -1.0, jnp.where(offset == -2, 1.0, 0.0))
    return (one + two).astype(jnp.bfloat16)


def split(value):
    high = value.astype(jnp.bfloat16)
    return high, (value - high.astype(jnp.float32)).astype(jnp.bfloat16)


def dot(a, b):
    return jnp.dot(a, b, preferred_element_type=jnp.float32)


def emit(sample, base, lin, grad_z, depth_step, through, position):
    root = lax.rsqrt(base + grad_z * grad_z * (1.0 / 144.0))
    diffuse = 0.3 + jnp.maximum((lin + grad_z * (0.64 * 0.7 / 12.0)) * root, 0.0)
    grown = jnp.exp(sample)
    optical = jnp.log(1.0 + grown) * ((2.0 - root * root) * depth_step)
    behind = through * jnp.exp(-optical)
    weight = through - behind
    lit = weight * diffuse
    square = grown * grown
    blue = lit / (1.0 + square)
    return behind, (blue * square, lit * jnp.exp(-0.5 * sample * sample), blue, weight * position)


def inner_kernel(ids, x_ref, ya_ref, yb_ref, e_ref, image_ref, part_ref, gx_ref, gy_ref, *, total_z, last_y):
    cells_z, rows, cols = x_ref.shape
    strip = e_ref.shape[2]
    depth_step = 2.0 / total_z
    at_x, at_y, at_z = ids[0], ids[1], ids[2]
    even = at_y % 2 == 0
    iota = functools.partial(lax.broadcasted_iota, jnp.int32)
    along_x = band(iota((cols, cols), 0) - iota((cols, cols), 1))
    lane = iota((strip, cols), 0) - iota((strip, cols), 1)
    beyond_x = jnp.where(at_x == 0, band(lane + cols), band(lane - strip))
    along_y = band(iota((rows, rows), 1) - iota((rows, rows), 0))
    out_row, slot = iota((rows, 2 * EDGE), 0), iota((rows, 2 * EDGE), 1)
    below = (slot < EDGE) == even
    cell = slot % EDGE
    beyond_y = band(jnp.where(below, rows + cell, cell - EDGE) - out_row)
    there = jnp.where(below, (at_y < last_y).astype(jnp.int32), (at_y > 0).astype(jnp.int32))
    beyond_y = jnp.where(there > 0, beyond_y, jnp.zeros_like(beyond_y))

    def gradients(k):
        high, low = split(x_ref[k])
        edge_high, edge_low = split(e_ref[k])
        gx_ref[...] = (
            dot(high, along_x) + dot(low, along_x)
            + dot(edge_high, beyond_x) + dot(edge_low, beyond_x)
        )
        rim_high, rim_low = split(jnp.concatenate([ya_ref[k], yb_ref[k]], axis=0))
        gy_ref[...] = (
            dot(along_y, high) + dot(along_y, low)
            + dot(beyond_y, rim_high) + dot(beyond_y, rim_low)
        )

    def pair(at):
        grad_x, grad_y = gx_ref[at], gy_ref[at]
        base = 1.0 + (grad_x * grad_x + grad_y * grad_y) * (1.0 / 144.0)
        lin = grad_x * (0.48 * 0.7 / 12.0) + grad_y * (0.6 * 0.7 / 12.0)
        return base, lin

    chunk = 16
    spans = [pl.ds(r, chunk) for r in range(0, rows, chunk)]
    for index, k in enumerate((0, 1, cells_z - 2, cells_z - 1)):
        gradients(k)
        for at in spans:
            base, lin = pair(at)
            part_ref[index, 0, at] = base
            part_ref[index, 1, at] = lin

    for channel in range(4):
        image_ref[channel] = jnp.zeros((rows, cols), jnp.float32)
    image_ref[4] = jnp.ones((rows, cols), jnp.float32)

    @pl.loop(2, cells_z - 2)
    def _(k):
        gradients(k)
        position = ((at_z * cells_z + k).astype(jnp.float32) + 0.5) / total_z
        for at in spans:
            base, lin = pair(at)
            grad_z = (x_ref[k - 2, at] - x_ref[k + 2, at]) + 8.0 * (x_ref[k + 1, at] - x_ref[k - 1, at])
            through, adds = emit(x_ref[k, at], base, lin, grad_z, depth_step, image_ref[4, at], position)
            image_ref[4, at] = through
            for channel, value in enumerate(adds):
                image_ref[channel, at] += value


def outer_kernel(ids, blocks, front_ref, back_ref, za_ref, zb_ref, image_ref, part_ref, *out_refs, total_z, cells_z):
    depth_step = 2.0 / total_z
    at_z = ids[2]
    last_z = total_z // cells_z - 1
    even = at_z % 2 == 0
    none = jnp.zeros(za_ref.shape[1:], jnp.float32)

    def before(layer):
        value = jnp.where(even, zb_ref[layer], za_ref[layer])
        return jnp.where(at_z > 0, value, none)

    def after(layer):
        value = jnp.where(even, za_ref[layer], zb_ref[layer])
        return jnp.where(at_z < last_z, value, none)

    f = front_ref
    b = back_ref
    ahead, next_ahead = before(0), before(1)
    behind, next_behind = after(0), after(1)
    cells = (
        (0, 0, f[0], (ahead - f[2]) + 8.0 * (f[1] - next_ahead)),
        (1, 1, f[1], (next_ahead - f[3]) + 8.0 * (f[2] - f[0])),
        (2, cells_z - 2, b[2], (b[0] - behind) + 8.0 * (b[3] - b[1])),
        (3, cells_z - 1, b[3], (b[1] - next_behind) + 8.0 * (behind - b[2])),
    )
    through = jnp.ones_like(none)
    sums = [jnp.zeros_like(none)] * 4
    for index, k, sample, grad_z in cells:
        if index == 2:
            sums = [s + through * image_ref[c] for c, s in enumerate(sums)]
            through = through * image_ref[4]
        position = ((at_z * cells_z + k).astype(jnp.float32) + 0.5) / total_z
        through, adds = emit(
            sample, part_ref[index, 0], part_ref[index, 1], grad_z, depth_step, through, position
        )
        sums = [s + a for s, a in zip(sums, adds)]
    image = sums + [through]
    for step, out_ref in enumerate(out_refs):

        @pl.when(pl.program_id(0) == step)
        def _():
            for channel, value in enumerate(image):
                out_ref[channel] = value


def join(front, back):
    through = front[4]
    return [front[c] + through * back[c] for c in range(4)] + [through * back[4]]


def put(image, colour_ref, depth_ref, clear_ref):
    for channel in range(3):
        colour_ref[channel] = image[channel]
    depth_ref[...] = image[3]
    clear_ref[...] = image[4]


def blend_four(ids, own_ref, one_ref, two_ref, three_ref, colour_ref, depth_ref, clear_ref):
    at_z = ids[2]
    odd, high = at_z % 2 == 1, at_z >= 2
    own, one, two, three = (
        [ref[c] for c in range(5)] for ref in (own_ref, one_ref, two_ref, three_ref)
    )

    def ordered(swap, a, b):
        front = [jnp.where(swap, q, p) for p, q in zip(a, b)]
        back = [jnp.where(swap, p, q) for p, q in zip(a, b)]
        return join(front, back)

    mine = ordered(odd, own, one)
    other = ordered(odd, two, three)
    put(ordered(high, mine, other), colour_ref, depth_ref, clear_ref)


def blend_all(parts_ref, colour_ref, depth_ref, clear_ref):
    image = [parts_ref[0, c] for c in range(5)]
    for k in range(1, parts_ref.shape[0]):
        image = join(image, [parts_ref[k, c] for c in range(5)])
    put(image, colour_ref, depth_ref, clear_ref)


def pairs(count):
    first = [(i, i ^ 1) for i in range(count)]
    second = [(i, (i - 1 if i % 2 == 0 else i + 1)) for i in range(1, count - 1)]
    return first, second + [(0, 0), (count - 1, count - 1)]


def exchange(block, axis, dim, width):
    length = block.shape[dim]
    even = lax.axis_index(axis) % 2 == 0
    first, second = pairs(lax.axis_size(axis))
    low, high = 0, length - width
    one = lax.dynamic_slice_in_dim(block, jnp.where(even, high, low), width, dim)
    two = lax.dynamic_slice_in_dim(block, jnp.where(even, low, high), width, dim)
    return lax.ppermute(one, axis, first), lax.ppermute(two, axis, second)


def on_device(block):
    cells_z, rows, cols = block.shape
    count_z = lax.axis_size("gz")
    total_z = cells_z * count_z
    at_x, at_y, at_z = (lax.axis_index(a) for a in ("gx", "gy", "gz"))
    ids = jnp.stack([at_x, at_y, at_z]).astype(jnp.int32)
    piece = rows // count_z
    strip = 128

    za, zb = exchange(block, "gz", 0, 2)
    ya, yb = exchange(block, "gy", 1, EDGE)
    edge = lax.dynamic_slice_in_dim(block, jnp.where(at_x == 0, cols - strip, 0), strip, 2)
    edge = lax.ppermute(edge, "gx", [(0, 1), (1, 0)])

    smem = pl.BlockSpec(memory_space=pltpu.SMEM)
    vmem = pl.BlockSpec(memory_space=pltpu.VMEM)
    params = pltpu.CompilerParams(vmem_limit_bytes=40 * 1024 * 1024)
    f32 = jnp.float32
    image, part = pl.pallas_call(
        functools.partial(inner_kernel, total_z=total_z, last_y=lax.axis_size("gy") - 1),
        out_shape=(
            jax.ShapeDtypeStruct((5, rows, cols), f32),
            jax.ShapeDtypeStruct((4, 2, rows, cols), f32),
        ),
        in_specs=[smem, vmem, vmem, vmem, vmem],
        out_specs=(vmem, vmem),
        scratch_shapes=[pltpu.VMEM((rows, cols), f32), pltpu.VMEM((rows, cols), f32)],
        compiler_params=params,
        cost_estimate=pl.CostEstimate(
            flops=100 * block.size, bytes_accessed=8 * block.size, transcendentals=6 * block.size
        ),
        name="inner",
    )(ids, block, ya, yb, edge)

    four = count_z == 4
    if four:
        order = jnp.stack([at_z ^ 1, at_z ^ 2, at_z ^ 3, at_z]).astype(jnp.int32)
    else:
        order = jnp.arange(count_z, dtype=jnp.int32)
    layers = cells_z // 4
    out_specs = [pl.BlockSpec((5, piece, cols), lambda i, ids, order: (0, 0, 0))] * count_z
    parts = pl.pallas_call(
        functools.partial(outer_kernel, total_z=total_z, cells_z=cells_z),
        out_shape=[jax.ShapeDtypeStruct((5, piece, cols), f32)] * count_z,
        grid_spec=pltpu.PrefetchScalarGridSpec(
            num_scalar_prefetch=2,
            grid=(count_z,),
            in_specs=[
                pl.BlockSpec((4, piece, cols), lambda i, ids, order: (0, order[i], 0)),
                pl.BlockSpec((4, piece, cols), lambda i, ids, order: (layers - 1, order[i], 0)),
                pl.BlockSpec((2, piece, cols), lambda i, ids, order: (0, order[i], 0)),
                pl.BlockSpec((2, piece, cols), lambda i, ids, order: (0, order[i], 0)),
                pl.BlockSpec((5, piece, cols), lambda i, ids, order: (0, order[i], 0)),
                pl.BlockSpec((4, 2, piece, cols), lambda i, ids, order: (0, 0, order[i], 0)),
            ],
            out_specs=out_specs,
        ),
        compiler_params=params,
        name="outer",
    )(ids, order, block, block, za, zb, image, part)

    out_shape = (
        jax.ShapeDtypeStruct((3, piece, cols), f32),
        jax.ShapeDtypeStruct((piece, cols), f32),
        jax.ShapeDtypeStruct((piece, cols), f32),
    )
    if four:
        peers = [
            lax.ppermute(parts[s - 1], "gz", [(i, i ^ s) for i in range(count_z)]) for s in (1, 2, 3)
        ]
        return pl.pallas_call(
            blend_four,
            out_shape=out_shape,
            in_specs=[smem] + [vmem] * 4,
            out_specs=(vmem, vmem, vmem),
            name="blend",
        )(ids, parts[3], *peers)
    gathered = lax.all_to_all(jnp.stack(parts), "gz", split_axis=0, concat_axis=0, tiled=True)
    return pl.pallas_call(
        blend_all, out_shape=out_shape, in_specs=[vmem], out_specs=(vmem, vmem, vmem), name="blend"
    )(gathered)


def solution(mesh):
    return jax.shard_map(
        on_device,
        mesh=mesh,
        in_specs=(P("gz", "gy", "gx"),),
        out_specs=(P(None, ("gy", "gz"), "gx"), P(("gy", "gz"), "gx"), P(("gy", "gz"), "gx")),
        check_vma=False,
    )
```

```python
import functools

import jax
import jax.numpy as jnp
from jax import lax
from jax.experimental import pallas as pl
from jax.experimental.pallas import tpu as pltpu
from jax.sharding import PartitionSpec as P

EDGE = 8


def band(offset):
    one = jnp.where(offset == 1, 8.0, jnp.where(offset == -1, -8.0, 0.0))
    two = jnp.where(offset == 2, -1.0, jnp.where(offset == -2, 1.0, 0.0))
    return (one + two).astype(jnp.bfloat16)


def split(value):
    high = value.astype(jnp.bfloat16)
    return high, (value - high.astype(jnp.float32)).astype(jnp.bfloat16)


def dot(a, b):
    return jnp.dot(a, b, preferred_element_type=jnp.float32)


def emit(sample, base, lin, grad_z, depth_step, through, position):
    root = lax.rsqrt(base + grad_z * grad_z * (1.0 / 144.0))
    diffuse = 0.3 + jnp.maximum((lin + grad_z * (0.64 * 0.7 / 12.0)) * root, 0.0)
    grown = jnp.exp(sample)
    optical = jnp.log(1.0 + grown) * ((2.0 - root * root) * depth_step)
    behind = through * jnp.exp(-optical)
    weight = through - behind
    lit = weight * diffuse
    square = grown * grown
    blue = lit / (1.0 + square)
    return behind, (blue * square, lit * jnp.exp(-0.5 * sample * sample), blue, weight * position)


def place():
    return tuple(lax.axis_index(a) for a in ("gx", "gy", "gz"))


def edges_kernel(x_ref, za_ref, zb_ref, ya_ref, yb_ref, e_ref, sems):
    cells_z, rows, cols = x_ref.shape
    at_x, at_y, at_z = place()
    strip = e_ref.shape[2]

    def starts(position, low, high):
        even = position % 2 == 0
        return jnp.where(even, high, low), jnp.where(even, low, high)

    z_one, z_two = starts(at_z, 0, cells_z - 2)
    y_one, y_two = (pl.multiple_of(v, EDGE) for v in starts(at_y, 0, rows - EDGE))
    x_one = pl.multiple_of(jnp.where(at_x == 0, cols - strip, 0), strip)
    copies = [
        pltpu.make_async_copy(x_ref.at[pl.ds(z_one, 2)], za_ref, sems.at[0]),
        pltpu.make_async_copy(x_ref.at[pl.ds(z_two, 2)], zb_ref, sems.at[1]),
        pltpu.make_async_copy(x_ref.at[:, pl.ds(y_one, EDGE)], ya_ref, sems.at[2]),
        pltpu.make_async_copy(x_ref.at[:, pl.ds(y_two, EDGE)], yb_ref, sems.at[3]),
        pltpu.make_async_copy(x_ref.at[:, :, pl.ds(x_one, strip)], e_ref, sems.at[4]),
    ]
    for copy in copies:
        copy.start()
    for copy in copies:
        copy.wait()


def inner_kernel(
    x_ref, ya_ref, yb_ref, e_ref, image_ref, part_ref, gx0, gx1, gy0, gy1, wx_ref, wy_ref, *, total_z, last_y
):
    cells_z, rows, cols = x_ref.shape
    strip = e_ref.shape[2]
    depth_step = 2.0 / total_z
    at_x, at_y, at_z = place()
    even = at_y % 2 == 0
    iota = functools.partial(lax.broadcasted_iota, jnp.int32)
    along_x = band(iota((cols, cols), 0) - iota((cols, cols), 1))
    lane = iota((strip, cols), 0) - iota((strip, cols), 1)
    beyond_x = band(lane + jnp.where(at_x == 0, cols, -strip))
    along_y = band(iota((rows, rows), 1) - iota((rows, rows), 0))
    out_row, slot = iota((rows, 2 * EDGE), 0), iota((rows, 2 * EDGE), 1)
    first = slot < EDGE
    cell = slot % EDGE
    below = jnp.where(first, even.astype(jnp.int32), 1 - even.astype(jnp.int32)) > 0
    top = jnp.where(at_y > 0, -EDGE, -4 * EDGE)
    bottom = jnp.where(at_y < last_y, rows, rows + 4 * EDGE)
    beyond_y = band(cell + jnp.where(below, bottom, top) - out_row)
    wx_ref[...] = jnp.concatenate([along_x, along_x, beyond_x, beyond_x], axis=0)
    wy_ref[...] = jnp.concatenate([along_y, along_y, beyond_y, beyond_y], axis=1)

    def gradients(k, gx_ref, gy_ref):
        high, low = split(x_ref[k])
        edge_high, edge_low = split(e_ref[k])
        rim_high, rim_low = split(jnp.concatenate([ya_ref[k], yb_ref[k]], axis=0))
        gx_ref[...] = dot(jnp.concatenate([high, low, edge_high, edge_low], axis=1), wx_ref[...])
        gy_ref[...] = dot(wy_ref[...], jnp.concatenate([high, low, rim_high, rim_low], axis=0))

    def pair(at, gx_ref, gy_ref):
        grad_x, grad_y = gx_ref[at], gy_ref[at]
        base = 1.0 + (grad_x * grad_x + grad_y * grad_y) * (1.0 / 144.0)
        lin = grad_x * (0.48 * 0.7 / 12.0) + grad_y * (0.6 * 0.7 / 12.0)
        return base, lin

    chunk = 16
    spans = [pl.ds(r, chunk) for r in range(0, rows, chunk)]
    slots = ((gx0, gy0), (gx1, gy1))

    def keep(index, pairs):
        for at in spans:
            base, lin = pair(at, *pairs)
            part_ref[index, 0, at] = base
            part_ref[index, 1, at] = lin

    def shade(k, pairs):
        position = ((at_z * cells_z + k).astype(jnp.float32) + 0.5) / total_z
        for at in spans:
            base, lin = pair(at, *pairs)
            grad_z = (x_ref[k - 2, at] - x_ref[k + 2, at]) + 8.0 * (x_ref[k + 1, at] - x_ref[k - 1, at])
            through, adds = emit(x_ref[k, at], base, lin, grad_z, depth_step, image_ref[4, at], position)
            image_ref[4, at] = through
            for channel, value in enumerate(adds):
                image_ref[channel, at] += value

    for channel in range(4):
        image_ref[channel] = jnp.zeros((rows, cols), jnp.float32)
    image_ref[4] = jnp.ones((rows, cols), jnp.float32)

    gradients(0, *slots[0])
    gradients(1, *slots[1])
    keep(0, slots[0])
    gradients(2, *slots[0])
    keep(1, slots[1])

    @pl.loop(0, (cells_z - 4) // 2)
    def _(step):
        k = 2 + 2 * step
        gradients(k + 1, *slots[1])
        shade(k, slots[0])
        gradients(k + 2, *slots[0])
        shade(k + 1, slots[1])

    gradients(cells_z - 1, *slots[1])
    keep(2, slots[0])
    keep(3, slots[1])


def outer_kernel(x_ref, za_ref, zb_ref, image_ref, part_ref, *out_refs, total_z):
    cells_z, _, cols = x_ref.shape
    depth_step = 2.0 / total_z
    at_z = place()[2]
    last_z = total_z // cells_z - 1
    even = at_z % 2 == 0
    count, piece = len(out_refs), out_refs[0].shape[1]
    chunk = min(piece, 16)
    none = jnp.zeros((chunk, cols), jnp.float32)
    for out, start in [(o, s) for o in range(count) for s in range(0, piece, chunk)]:
        block = at_z ^ out if count == 4 else out
        at = pl.ds(pl.multiple_of(block * piece + start, 8), chunk)

        def before(layer):
            return jnp.where(at_z > 0, jnp.where(even, zb_ref[layer, at], za_ref[layer, at]), none)

        def after(layer):
            return jnp.where(at_z < last_z, jnp.where(even, za_ref[layer, at], zb_ref[layer, at]), none)

        f = [x_ref[k, at] for k in range(4)]
        b = [x_ref[cells_z - 4 + k, at] for k in range(4)]
        ahead, next_ahead, behind, next_behind = before(0), before(1), after(0), after(1)
        cells = (
            (0, 0, f[0], (ahead - f[2]) + 8.0 * (f[1] - next_ahead)),
            (1, 1, f[1], (next_ahead - f[3]) + 8.0 * (f[2] - f[0])),
            (2, cells_z - 2, b[2], (b[0] - behind) + 8.0 * (b[3] - b[1])),
            (3, cells_z - 1, b[3], (b[1] - next_behind) + 8.0 * (behind - b[2])),
        )
        through = jnp.ones_like(none)
        sums = [none] * 4
        for index, k, sample, grad_z in cells:
            if index == 2:
                sums = [s + through * image_ref[c, at] for c, s in enumerate(sums)]
                through = through * image_ref[4, at]
            position = ((at_z * cells_z + k).astype(jnp.float32) + 0.5) / total_z
            through, adds = emit(
                sample, part_ref[index, 0, at], part_ref[index, 1, at], grad_z, depth_step, through, position
            )
            sums = [s + a for s, a in zip(sums, adds)]
        for channel, value in enumerate(sums + [through]):
            out_refs[out][channel, pl.ds(start, chunk)] = value


def join(front, back):
    through = front[4]
    return [front[c] + through * back[c] for c in range(4)] + [through * back[4]]


def put(image, colour_ref, depth_ref, clear_ref):
    for channel in range(3):
        colour_ref[channel] = image[channel]
    depth_ref[...] = image[3]
    clear_ref[...] = image[4]


def blend_four(own_ref, one_ref, two_ref, three_ref, colour_ref, depth_ref, clear_ref):
    at_z = place()[2]
    odd, high = at_z % 2 == 1, at_z >= 2
    own, one, two, three = (
        [ref[c] for c in range(5)] for ref in (own_ref, one_ref, two_ref, three_ref)
    )

    def ordered(swap, a, b):
        front = [jnp.where(swap, q, p) for p, q in zip(a, b)]
        back = [jnp.where(swap, p, q) for p, q in zip(a, b)]
        return join(front, back)

    mine = ordered(odd, own, one)
    other = ordered(odd, two, three)
    put(ordered(high, mine, other), colour_ref, depth_ref, clear_ref)


def blend_all(parts_ref, colour_ref, depth_ref, clear_ref):
    image = [parts_ref[0, c] for c in range(5)]
    for k in range(1, parts_ref.shape[0]):
        image = join(image, [parts_ref[k, c] for c in range(5)])
    put(image, colour_ref, depth_ref, clear_ref)


def pairs(count, closed):
    ends = [(0, count - 1), (count - 1, 0)] if closed else [(0, 0), (count - 1, count - 1)]
    first = [(i, i ^ 1) for i in range(count)]
    second = [(i, (i - 1 if i % 2 == 0 else i + 1)) for i in range(1, count - 1)]
    return first, second + ends


def on_device(block):
    cells_z, rows, cols = block.shape
    count_z, count_y = lax.axis_size("gz"), lax.axis_size("gy")
    total_z = cells_z * count_z
    piece = rows // count_z
    strip = 128
    f32 = jnp.float32

    def shaped(*shape):
        return jax.ShapeDtypeStruct(shape, f32)

    vmem = pl.BlockSpec(memory_space=pltpu.VMEM)
    edges = pl.pallas_call(
        edges_kernel,
        out_shape=(
            shaped(2, rows, cols), shaped(2, rows, cols),
            shaped(cells_z, EDGE, cols), shaped(cells_z, EDGE, cols),
            shaped(cells_z, rows, strip),
        ),
        in_specs=[pl.BlockSpec(memory_space=pltpu.HBM)],
        out_specs=(vmem,) * 5,
        scratch_shapes=[pltpu.SemaphoreType.DMA((5,))],
        compiler_params=pltpu.CompilerParams(vmem_limit_bytes=4 * 1024 * 1024),
        name="edges",
    )(block)
    z_first, z_second = pairs(count_z, False)
    y_first, y_second = pairs(count_y, True)
    za = lax.ppermute(edges[0], "gz", z_first)
    zb = lax.ppermute(edges[1], "gz", z_second)
    ya = lax.ppermute(edges[2], "gy", y_first)
    yb = lax.ppermute(edges[3], "gy", y_second)
    edge = lax.ppermute(edges[4], "gx", [(0, 1), (1, 0)])

    image, part = pl.pallas_call(
        functools.partial(inner_kernel, total_z=total_z, last_y=count_y - 1),
        out_shape=(shaped(5, rows, cols), shaped(4, 2, rows, cols)),
        in_specs=[vmem] * 4,
        out_specs=(vmem, vmem),
        scratch_shapes=[pltpu.VMEM((rows, cols), f32)] * 4
        + [
            pltpu.VMEM((2 * (cols + strip), cols), jnp.bfloat16),
            pltpu.VMEM((rows, 2 * (rows + 2 * EDGE)), jnp.bfloat16),
        ],
        compiler_params=pltpu.CompilerParams(vmem_limit_bytes=16 * 1024 * 1024),
        cost_estimate=pl.CostEstimate(
            flops=100 * block.size, bytes_accessed=8 * block.size, transcendentals=6 * block.size
        ),
        name="inner",
    )(block, ya, yb, edge)

    parts = pl.pallas_call(
        functools.partial(outer_kernel, total_z=total_z),
        out_shape=[shaped(5, piece, cols)] * count_z,
        in_specs=[vmem] * 5,
        out_specs=[vmem] * count_z,
        compiler_params=pltpu.CompilerParams(vmem_limit_bytes=16 * 1024 * 1024),
        name="outer",
    )(block, za, zb, image, part)

    out_shape = (shaped(3, piece, cols), shaped(piece, cols), shaped(piece, cols))
    small = pltpu.CompilerParams(vmem_limit_bytes=8 * 1024 * 1024)
    if count_z == 4:
        peers = [
            lax.ppermute(parts[s], "gz", [(i, i ^ s) for i in range(count_z)]) for s in (1, 2, 3)
        ]
        return pl.pallas_call(
            blend_four,
            out_shape=out_shape,
            in_specs=[vmem] * 4,
            out_specs=(vmem, vmem, vmem),
            compiler_params=small,
            name="blend",
        )(parts[0], *peers)
    gathered = lax.all_to_all(jnp.stack(parts), "gz", split_axis=0, concat_axis=0, tiled=True)
    return pl.pallas_call(
        blend_all,
        out_shape=out_shape,
        in_specs=[vmem],
        out_specs=(vmem, vmem, vmem),
        compiler_params=small,
        name="blend",
    )(gathered)


def solution(mesh):
    return jax.shard_map(
        on_device,
        mesh=mesh,
        in_specs=(P("gz", "gy", "gx"),),
        out_specs=(P(None, ("gy", "gz"), "gx"), P(("gy", "gz"), "gx"), P(("gy", "gz"), "gx")),
        check_vma=False,
    )
```

```python
import functools

import jax
import jax.numpy as jnp
from jax import lax
from jax.experimental import pallas as pl
from jax.experimental.pallas import tpu as pltpu
from jax.sharding import PartitionSpec as P

HALO = 2


def band(offset):
    one = jnp.where(offset == 1, 8.0, jnp.where(offset == -1, -8.0, 0.0))
    two = jnp.where(offset == 2, -1.0, jnp.where(offset == -2, 1.0, 0.0))
    return (one + two).astype(jnp.bfloat16)


def split(value):
    high = value.astype(jnp.bfloat16)
    return high, (value - high.astype(jnp.float32)).astype(jnp.bfloat16)


def dot(a, b):
    return jnp.dot(a, b, preferred_element_type=jnp.float32)


def emit(sample, base, lin, grad_z, depth_step, through, position):
    root = lax.rsqrt(base + grad_z * grad_z * (1.0 / 144.0))
    diffuse = 0.3 + jnp.maximum((lin + grad_z * (0.64 * 0.7 / 12.0)) * root, 0.0)
    grown = jnp.exp(sample)
    optical = jnp.log(1.0 + grown) * ((2.0 - root * root) * depth_step)
    behind = through * jnp.exp(-optical)
    weight = through - behind
    lit = weight * diffuse
    square = grown * grown
    blue = lit / (1.0 + square)
    return behind, (blue * square, lit * jnp.exp(-0.5 * sample * sample), blue, weight * position)


def place():
    return tuple(lax.axis_index(a) for a in ("gx", "gy", "gz"))


def edges_kernel(x_ref, za_ref, zb_ref, ya_ref, yb_ref, e_ref, sems):
    cells_z, rows, cols = x_ref.shape
    at_x, at_y, at_z = place()
    strip = e_ref.shape[2]
    even_z, even_y = at_z % 2 == 0, at_y % 2 == 0
    high = cells_z - HALO
    x_one = pl.multiple_of(jnp.where(at_x == 0, cols - strip, 0), strip)
    copies = [
        pltpu.make_async_copy(x_ref.at[pl.ds(jnp.where(even_z, high, 0), HALO)], za_ref, sems.at[0]),
        pltpu.make_async_copy(x_ref.at[pl.ds(jnp.where(even_z, 0, high), HALO)], zb_ref, sems.at[1]),
        pltpu.make_async_copy(x_ref.at[:, :, pl.ds(x_one, strip)], e_ref, sems.at[2]),
    ]
    for copy in copies:
        copy.start()
    top, bottom = x_ref[:, :HALO, :], x_ref[:, rows - HALO :, :]
    ya_ref[...] = jnp.where(even_y, bottom, top)
    yb_ref[...] = jnp.where(even_y, top, bottom)
    for copy in copies:
        copy.wait()


def inner_kernel(
    x_ref, ya_ref, yb_ref, e_ref, image_ref, part_ref, gx0, gx1, gy0, gy1, wx_ref, wy_ref, rim_ref, *, total_z, last_y
):
    cells_z, rows, cols = x_ref.shape
    strip = e_ref.shape[2]
    depth_step = 2.0 / total_z
    at_x, at_y, at_z = place()
    even = at_y % 2 == 0
    iota = functools.partial(lax.broadcasted_iota, jnp.int32)
    along_x = band(iota((cols, cols), 0) - iota((cols, cols), 1))
    lane = iota((strip, cols), 0) - iota((strip, cols), 1)
    beyond_x = band(lane + jnp.where(at_x == 0, cols, -strip))
    along_y = band(iota((rows, rows), 1) - iota((rows, rows), 0))
    out_row, slot = iota((rows, 4 * HALO), 0), iota((rows, 4 * HALO), 1)
    none = rows * 4
    top = jnp.where(at_y > 0, -HALO, none)
    bottom = jnp.where(at_y < last_y, rows, none)
    offset = jnp.where(
        slot < HALO,
        slot + jnp.where(even, bottom, top),
        slot - HALO + jnp.where(even, top, bottom),
    )
    beyond_y = band(jnp.where(slot < 2 * HALO, offset, none) - out_row)
    rim_ref[:, :HALO, :] = ya_ref[...]
    rim_ref[:, HALO : 2 * HALO, :] = yb_ref[...]
    rim_ref[:, 2 * HALO :, :] = jnp.zeros((cells_z, 2 * HALO, cols), jnp.float32)
    wx_ref[...] = jnp.concatenate([along_x, along_x, beyond_x, beyond_x], axis=0)
    wy_ref[...] = jnp.concatenate([along_y, along_y, beyond_y, beyond_y], axis=1)

    def gradients(k, gx_ref, gy_ref):
        high, low = split(x_ref[k])
        edge_high, edge_low = split(e_ref[k])
        rim_high, rim_low = split(rim_ref[k])
        gx_ref[...] = dot(jnp.concatenate([high, low, edge_high, edge_low], axis=1), wx_ref[...])
        gy_ref[...] = dot(wy_ref[...], jnp.concatenate([high, low, rim_high, rim_low], axis=0))

    def pair(at, gx_ref, gy_ref):
        grad_x, grad_y = gx_ref[at], gy_ref[at]
        base = 1.0 + (grad_x * grad_x + grad_y * grad_y) * (1.0 / 144.0)
        lin = grad_x * (0.48 * 0.7 / 12.0) + grad_y * (0.6 * 0.7 / 12.0)
        return base, lin

    chunk = 16
    spans = [pl.ds(r, chunk) for r in range(0, rows, chunk)]
    slots = ((gx0, gy0), (gx1, gy1))

    def keep(index, pairs):
        for at in spans:
            base, lin = pair(at, *pairs)
            part_ref[index, 0, at] = base
            part_ref[index, 1, at] = lin

    def shade(k, pairs):
        position = ((at_z * cells_z + k).astype(jnp.float32) + 0.5) / total_z
        for at in spans:
            base, lin = pair(at, *pairs)
            grad_z = (x_ref[k - 2, at] - x_ref[k + 2, at]) + 8.0 * (x_ref[k + 1, at] - x_ref[k - 1, at])
            through, adds = emit(x_ref[k, at], base, lin, grad_z, depth_step, image_ref[4, at], position)
            image_ref[4, at] = through
            for channel, value in enumerate(adds):
                image_ref[channel, at] += value

    for channel in range(4):
        image_ref[channel] = jnp.zeros((rows, cols), jnp.float32)
    image_ref[4] = jnp.ones((rows, cols), jnp.float32)

    gradients(0, *slots[0])
    gradients(1, *slots[1])
    keep(0, slots[0])
    gradients(2, *slots[0])
    keep(1, slots[1])

    @pl.loop(0, (cells_z - 4) // 2)
    def _(step):
        k = 2 + 2 * step
        gradients(k + 1, *slots[1])
        shade(k, slots[0])
        gradients(k + 2, *slots[0])
        shade(k + 1, slots[1])

    gradients(cells_z - 1, *slots[1])
    keep(2, slots[0])
    keep(3, slots[1])


def outer_kernel(x_ref, za_ref, zb_ref, image_ref, part_ref, *out_refs, total_z):
    cells_z, _, cols = x_ref.shape
    depth_step = 2.0 / total_z
    at_z = place()[2]
    last_z = total_z // cells_z - 1
    even = at_z % 2 == 0
    count, piece = len(out_refs), out_refs[0].shape[1]
    chunk = min(piece, 16)
    none = jnp.zeros((chunk, cols), jnp.float32)
    for out, start in [(o, s) for o in range(count) for s in range(0, piece, chunk)]:
        block = at_z ^ out if count == 4 else out
        at = pl.ds(pl.multiple_of(block * piece + start, 8), chunk)

        def before(layer):
            return jnp.where(at_z > 0, jnp.where(even, zb_ref[layer, at], za_ref[layer, at]), none)

        def after(layer):
            return jnp.where(at_z < last_z, jnp.where(even, za_ref[layer, at], zb_ref[layer, at]), none)

        f = [x_ref[k, at] for k in range(4)]
        b = [x_ref[cells_z - 4 + k, at] for k in range(4)]
        ahead, next_ahead, behind, next_behind = before(0), before(1), after(0), after(1)
        cells = (
            (0, 0, f[0], (ahead - f[2]) + 8.0 * (f[1] - next_ahead)),
            (1, 1, f[1], (next_ahead - f[3]) + 8.0 * (f[2] - f[0])),
            (2, cells_z - 2, b[2], (b[0] - behind) + 8.0 * (b[3] - b[1])),
            (3, cells_z - 1, b[3], (b[1] - next_behind) + 8.0 * (behind - b[2])),
        )
        through = jnp.ones_like(none)
        sums = [none] * 4
        for index, k, sample, grad_z in cells:
            if index == 2:
                sums = [s + through * image_ref[c, at] for c, s in enumerate(sums)]
                through = through * image_ref[4, at]
            position = ((at_z * cells_z + k).astype(jnp.float32) + 0.5) / total_z
            through, adds = emit(
                sample, part_ref[index, 0, at], part_ref[index, 1, at], grad_z, depth_step, through, position
            )
            sums = [s + a for s, a in zip(sums, adds)]
        for channel, value in enumerate(sums + [through]):
            out_refs[out][channel, pl.ds(start, chunk)] = value


def join(front, back):
    through = front[4]
    return [front[c] + through * back[c] for c in range(4)] + [through * back[4]]


def put(image, colour_ref, depth_ref, clear_ref):
    for channel in range(3):
        colour_ref[channel] = image[channel]
    depth_ref[...] = image[3]
    clear_ref[...] = image[4]


def blend_four(own_ref, one_ref, two_ref, three_ref, colour_ref, depth_ref, clear_ref):
    at_z = place()[2]
    odd, high = at_z % 2 == 1, at_z >= 2
    own, one, two, three = (
        [ref[c] for c in range(5)] for ref in (own_ref, one_ref, two_ref, three_ref)
    )

    def ordered(swap, a, b):
        front = [jnp.where(swap, q, p) for p, q in zip(a, b)]
        back = [jnp.where(swap, p, q) for p, q in zip(a, b)]
        return join(front, back)

    mine = ordered(odd, own, one)
    other = ordered(odd, two, three)
    put(ordered(high, mine, other), colour_ref, depth_ref, clear_ref)


def blend_all(parts_ref, colour_ref, depth_ref, clear_ref):
    image = [parts_ref[0, c] for c in range(5)]
    for k in range(1, parts_ref.shape[0]):
        image = join(image, [parts_ref[k, c] for c in range(5)])
    put(image, colour_ref, depth_ref, clear_ref)


def pairs(count, closed):
    ends = [(0, count - 1), (count - 1, 0)] if closed else [(0, 0), (count - 1, count - 1)]
    first = [(i, i ^ 1) for i in range(count)]
    second = [(i, (i - 1 if i % 2 == 0 else i + 1)) for i in range(1, count - 1)]
    return first, second + ends


def on_device(block):
    cells_z, rows, cols = block.shape
    count_z, count_y = lax.axis_size("gz"), lax.axis_size("gy")
    total_z = cells_z * count_z
    piece = rows // count_z
    strip = 128
    f32 = jnp.float32

    def shaped(*shape):
        return jax.ShapeDtypeStruct(shape, f32)

    vmem = pl.BlockSpec(memory_space=pltpu.VMEM)
    edges = pl.pallas_call(
        edges_kernel,
        out_shape=(
            shaped(HALO, rows, cols), shaped(HALO, rows, cols),
            shaped(cells_z, HALO, cols), shaped(cells_z, HALO, cols),
            shaped(cells_z, rows, strip),
        ),
        in_specs=[vmem],
        out_specs=(vmem,) * 5,
        scratch_shapes=[pltpu.SemaphoreType.DMA((3,))],
        compiler_params=pltpu.CompilerParams(vmem_limit_bytes=4 * 1024 * 1024),
        name="edges",
    )(block)
    z_first, z_second = pairs(count_z, False)
    y_first, y_second = pairs(count_y, True)
    za = lax.ppermute(edges[0], "gz", z_first)
    zb = lax.ppermute(edges[1], "gz", z_second)
    ya = lax.ppermute(edges[2], "gy", y_first)
    yb = lax.ppermute(edges[3], "gy", y_second)
    edge = lax.ppermute(edges[4], "gx", [(0, 1), (1, 0)])

    image, part = pl.pallas_call(
        functools.partial(inner_kernel, total_z=total_z, last_y=count_y - 1),
        out_shape=(shaped(5, rows, cols), shaped(4, 2, rows, cols)),
        in_specs=[vmem] * 4,
        out_specs=(vmem, vmem),
        scratch_shapes=[pltpu.VMEM((rows, cols), f32)] * 4
        + [
            pltpu.VMEM((2 * (cols + strip), cols), jnp.bfloat16),
            pltpu.VMEM((rows, 2 * (rows + 4 * HALO)), jnp.bfloat16),
            pltpu.VMEM((cells_z, 4 * HALO, cols), f32),
        ],
        compiler_params=pltpu.CompilerParams(vmem_limit_bytes=16 * 1024 * 1024),
        cost_estimate=pl.CostEstimate(
            flops=100 * block.size, bytes_accessed=8 * block.size, transcendentals=6 * block.size
        ),
        name="inner",
    )(block, ya, yb, edge)

    parts = pl.pallas_call(
        functools.partial(outer_kernel, total_z=total_z),
        out_shape=[shaped(5, piece, cols)] * count_z,
        in_specs=[vmem] * 5,
        out_specs=[vmem] * count_z,
        compiler_params=pltpu.CompilerParams(vmem_limit_bytes=16 * 1024 * 1024),
        name="outer",
    )(block, za, zb, image, part)

    out_shape = (shaped(3, piece, cols), shaped(piece, cols), shaped(piece, cols))
    small = pltpu.CompilerParams(vmem_limit_bytes=8 * 1024 * 1024)
    if count_z == 4:
        peers = [
            lax.ppermute(parts[s], "gz", [(i, i ^ s) for i in range(count_z)]) for s in (1, 2, 3)
        ]
        return pl.pallas_call(
            blend_four,
            out_shape=out_shape,
            in_specs=[vmem] * 4,
            out_specs=(vmem, vmem, vmem),
            compiler_params=small,
            name="blend",
        )(parts[0], *peers)
    gathered = lax.all_to_all(jnp.stack(parts), "gz", split_axis=0, concat_axis=0, tiled=True)
    return pl.pallas_call(
        blend_all,
        out_shape=out_shape,
        in_specs=[vmem],
        out_specs=(vmem, vmem, vmem),
        compiler_params=small,
        name="blend",
    )(gathered)


def solution(mesh):
    return jax.shard_map(
        on_device,
        mesh=mesh,
        in_specs=(P("gz", "gy", "gx"),),
        out_specs=(P(None, ("gy", "gz"), "gx"), P(("gy", "gz"), "gx"), P(("gy", "gz"), "gx")),
        check_vma=False,
    )
```

```python
import functools

import jax
import jax.numpy as jnp
from jax import lax
from jax.experimental import pallas as pl
from jax.experimental.pallas import tpu as pltpu
from jax.sharding import PartitionSpec as P

HALO = 2
RIM = 8


def band(offset):
    one = jnp.where(offset == 1, 8.0, jnp.where(offset == -1, -8.0, 0.0))
    two = jnp.where(offset == 2, -1.0, jnp.where(offset == -2, 1.0, 0.0))
    return (one + two).astype(jnp.bfloat16)


def split(value):
    high = value.astype(jnp.bfloat16)
    return high, (value - high.astype(jnp.float32)).astype(jnp.bfloat16)


def dot(a, b):
    return jnp.dot(a, b, preferred_element_type=jnp.float32)


def emit(sample, base, lin, grad_z, depth_step, through, position):
    root = lax.rsqrt(base + grad_z * grad_z * (1.0 / 144.0))
    diffuse = 0.3 + jnp.maximum((lin + grad_z * (0.64 * 0.7 / 12.0)) * root, 0.0)
    grown = jnp.exp(sample)
    optical = jnp.log(1.0 + grown) * ((2.0 - root * root) * depth_step)
    behind = through * jnp.exp(-optical)
    weight = through - behind
    lit = weight * diffuse
    square = grown * grown
    blue = lit / (1.0 + square)
    return behind, (blue * square, lit * jnp.exp(-0.5 * sample * sample), blue, weight * position)


def place():
    return tuple(lax.axis_index(a) for a in ("gx", "gy", "gz"))


def edges_kernel(x_ref, za_ref, zb_ref, ya_ref, yb_ref, e_ref, top_ref, bottom_ref, sems):
    cells_z, rows, cols = x_ref.shape
    at_x, at_y, at_z = place()
    strip = e_ref.shape[2]
    even_z, even_y = at_z % 2 == 0, at_y % 2 == 0
    high = cells_z - HALO
    start = pl.multiple_of(jnp.where(at_x == 0, cols - strip, 0), strip)
    copies = [
        pltpu.make_async_copy(source, target, sems.at[i])
        for i, (source, target) in enumerate(
            (
                (x_ref.at[pl.ds(jnp.where(even_z, high, 0), HALO)], za_ref),
                (x_ref.at[pl.ds(jnp.where(even_z, 0, high), HALO)], zb_ref),
                (x_ref.at[:, pl.ds(0, RIM)], top_ref),
                (x_ref.at[:, pl.ds(rows - RIM, RIM)], bottom_ref),
                (x_ref.at[:, :, pl.ds(start, strip)], e_ref),
            )
        )
    ]
    for copy in copies:
        copy.start()
    for copy in copies:
        copy.wait()
    top, bottom = top_ref[:, :HALO, :], bottom_ref[:, RIM - HALO :, :]
    ya_ref[...] = jnp.where(even_y, bottom, top)
    yb_ref[...] = jnp.where(even_y, top, bottom)


def pair(grad_x, grad_y):
    base = 1.0 + (grad_x * grad_x + grad_y * grad_y) * (1.0 / 144.0)
    lin = grad_x * (0.48 * 0.7 / 12.0) + grad_y * (0.6 * 0.7 / 12.0)
    return base, lin


def inner_kernel(
    x_ref, e_ref, image_ref, part_ref, rim_ref, gx0, gx1, gy0, gy1, wx_ref, wy_ref, *, total_z
):
    cells_z, rows, cols = x_ref.shape
    strip = e_ref.shape[2]
    depth_step = 2.0 / total_z
    at_x, _, at_z = place()
    iota = functools.partial(lax.broadcasted_iota, jnp.int32)
    along_x = band(iota((cols, cols), 0) - iota((cols, cols), 1))
    lane = iota((strip, cols), 0) - iota((strip, cols), 1)
    beyond_x = band(lane + jnp.where(at_x == 0, cols, -strip))
    along_y = band(iota((rows, rows), 1) - iota((rows, rows), 0))
    wx_ref[...] = jnp.concatenate([along_x, along_x, beyond_x, beyond_x], axis=0)
    wy_ref[...] = jnp.concatenate([along_y, along_y], axis=1)

    chunk = 16
    spans = [pl.ds(r, chunk) for r in range(RIM, rows - RIM, chunk)]
    slots = ((gx0, gy0), (gx1, gy1))

    def gradients(k, slot):
        high, low = split(x_ref[k])
        edge_high, edge_low = split(e_ref[k])
        for axis, value in enumerate(
            (
                dot(jnp.concatenate([high, low, edge_high, edge_low], axis=1), wx_ref[...]),
                dot(wy_ref[...], jnp.concatenate([high, low], axis=0)),
            )
        ):
            slots[slot][axis][...] = value
            rim_ref[k, axis, :RIM] = value[:RIM]
            rim_ref[k, axis, RIM:] = value[rows - RIM :]

    def keep(index, slot):
        grad_x, grad_y = slots[slot]
        for at in spans:
            part_ref[index, 0, at], part_ref[index, 1, at] = pair(grad_x[at], grad_y[at])

    def shade(k, slot):
        grad_x, grad_y = slots[slot]
        position = ((at_z * cells_z + k).astype(jnp.float32) + 0.5) / total_z
        for at in spans:
            base, lin = pair(grad_x[at], grad_y[at])
            grad_z = (x_ref[k - 2, at] - x_ref[k + 2, at]) + 8.0 * (x_ref[k + 1, at] - x_ref[k - 1, at])
            through, adds = emit(x_ref[k, at], base, lin, grad_z, depth_step, image_ref[4, at], position)
            image_ref[4, at] = through
            for channel, value in enumerate(adds):
                image_ref[channel, at] += value

    for channel in range(4):
        image_ref[channel] = jnp.zeros((rows, cols), jnp.float32)
    image_ref[4] = jnp.ones((rows, cols), jnp.float32)

    gradients(0, 0)
    gradients(1, 1)
    keep(0, 0)
    gradients(2, 0)
    keep(1, 1)

    @pl.loop(0, (cells_z - 4) // 2)
    def _(step):
        k = 2 + 2 * step
        gradients(k + 1, 1)
        shade(k, 0)
        gradients(k + 2, 0)
        shade(k + 1, 1)

    gradients(cells_z - 1, 1)
    keep(2, 0)
    keep(3, 1)


def rim_kernel(x_ref, ya_ref, yb_ref, rim_ref, image_in, part_in, image_ref, part_ref, *, total_z, last_y):
    del image_in, part_in
    cells_z, rows, cols = x_ref.shape
    depth_step = 2.0 / total_z
    _, at_y, at_z = place()
    even = at_y % 2 == 0
    row = lax.broadcasted_iota(jnp.int32, (RIM, cols), 0)
    zero = jnp.zeros((RIM, cols), jnp.float32)

    def weights(position, there):
        offset = position - row
        one = jnp.where(offset == 1, 8.0, jnp.where(offset == -1, -8.0, 0.0))
        two = jnp.where(offset == 2, -1.0, jnp.where(offset == -2, 1.0, 0.0))
        return jnp.where(there, one + two, zero)

    sides = (
        (0, 0, even, [weights(-HALO + i, at_y > 0) for i in range(HALO)]),
        (RIM, rows - RIM, ~even, [weights(RIM + i, at_y < last_y) for i in range(HALO)]),
    )
    for start, first_row, second, scale in sides:
        at, to = pl.ds(start, RIM), pl.ds(first_row, RIM)

        def planes(k):
            grad_y = rim_ref[k, 1, at]
            for i in range(HALO):
                cell = jnp.where(second, yb_ref[k, i : i + 1], ya_ref[k, i : i + 1])
                grad_y = grad_y + scale[i] * jnp.broadcast_to(cell, (RIM, cols))
            return pair(rim_ref[k, 0, at], grad_y)

        for index, k in enumerate((0, 1, cells_z - 2, cells_z - 1)):
            part_ref[index, 0, to], part_ref[index, 1, to] = planes(k)
        through, sums = zero + 1.0, [zero] * 4
        for k in range(2, cells_z - 2):
            position = ((at_z * cells_z + k).astype(jnp.float32) + 0.5) / total_z
            grad_z = (x_ref[k - 2, to] - x_ref[k + 2, to]) + 8.0 * (x_ref[k + 1, to] - x_ref[k - 1, to])
            base, lin = planes(k)
            through, adds = emit(x_ref[k, to], base, lin, grad_z, depth_step, through, position)
            sums = [s + a for s, a in zip(sums, adds)]
        for channel, value in enumerate(sums + [through]):
            image_ref[channel, to] = value


def outer_kernel(x_ref, za_ref, zb_ref, image_ref, part_ref, *out_refs, total_z):
    cells_z, _, cols = x_ref.shape
    depth_step = 2.0 / total_z
    at_z = place()[2]
    last_z = total_z // cells_z - 1
    even = at_z % 2 == 0
    count, piece = len(out_refs), out_refs[0].shape[1]
    chunk = min(piece, 16)
    none = jnp.zeros((chunk, cols), jnp.float32)
    for out, start in [(o, s) for o in range(count) for s in range(0, piece, chunk)]:
        block = at_z ^ out if count == 4 else out
        at = pl.ds(pl.multiple_of(block * piece + start, 8), chunk)

        def before(layer):
            return jnp.where(at_z > 0, jnp.where(even, zb_ref[layer, at], za_ref[layer, at]), none)

        def after(layer):
            return jnp.where(at_z < last_z, jnp.where(even, za_ref[layer, at], zb_ref[layer, at]), none)

        f = [x_ref[k, at] for k in range(4)]
        b = [x_ref[cells_z - 4 + k, at] for k in range(4)]
        ahead, next_ahead, behind, next_behind = before(0), before(1), after(0), after(1)
        cells = (
            (0, 0, f[0], (ahead - f[2]) + 8.0 * (f[1] - next_ahead)),
            (1, 1, f[1], (next_ahead - f[3]) + 8.0 * (f[2] - f[0])),
            (2, cells_z - 2, b[2], (b[0] - behind) + 8.0 * (b[3] - b[1])),
            (3, cells_z - 1, b[3], (b[1] - next_behind) + 8.0 * (behind - b[2])),
        )
        through = jnp.ones_like(none)
        sums = [none] * 4
        for index, k, sample, grad_z in cells:
            if index == 2:
                sums = [s + through * image_ref[c, at] for c, s in enumerate(sums)]
                through = through * image_ref[4, at]
            position = ((at_z * cells_z + k).astype(jnp.float32) + 0.5) / total_z
            through, adds = emit(
                sample, part_ref[index, 0, at], part_ref[index, 1, at], grad_z, depth_step, through, position
            )
            sums = [s + a for s, a in zip(sums, adds)]
        for channel, value in enumerate(sums + [through]):
            out_refs[out][channel, pl.ds(start, chunk)] = value


def join(front, back):
    through = front[4]
    return [front[c] + through * back[c] for c in range(4)] + [through * back[4]]


def put(image, colour_ref, depth_ref, clear_ref):
    for channel in range(3):
        colour_ref[channel] = image[channel]
    depth_ref[...] = image[3]
    clear_ref[...] = image[4]


def blend_four(own_ref, one_ref, two_ref, three_ref, colour_ref, depth_ref, clear_ref):
    at_z = place()[2]
    odd, high = at_z % 2 == 1, at_z >= 2
    own, one, two, three = (
        [ref[c] for c in range(5)] for ref in (own_ref, one_ref, two_ref, three_ref)
    )

    def ordered(swap, a, b):
        front = [jnp.where(swap, q, p) for p, q in zip(a, b)]
        back = [jnp.where(swap, p, q) for p, q in zip(a, b)]
        return join(front, back)

    mine = ordered(odd, own, one)
    other = ordered(odd, two, three)
    put(ordered(high, mine, other), colour_ref, depth_ref, clear_ref)


def blend_all(parts_ref, colour_ref, depth_ref, clear_ref):
    image = [parts_ref[0, c] for c in range(5)]
    for k in range(1, parts_ref.shape[0]):
        image = join(image, [parts_ref[k, c] for c in range(5)])
    put(image, colour_ref, depth_ref, clear_ref)


def pairs(count, closed):
    ends = [(0, count - 1), (count - 1, 0)] if closed else [(0, 0), (count - 1, count - 1)]
    first = [(i, i ^ 1) for i in range(count)]
    second = [(i, (i - 1 if i % 2 == 0 else i + 1)) for i in range(1, count - 1)]
    return first, second + ends


def on_device(block):
    cells_z, rows, cols = block.shape
    count_z, count_y = lax.axis_size("gz"), lax.axis_size("gy")
    total_z = cells_z * count_z
    piece = rows // count_z
    strip = 128
    f32 = jnp.float32

    def shaped(*shape):
        return jax.ShapeDtypeStruct(shape, f32)

    vmem = pl.BlockSpec(memory_space=pltpu.VMEM)
    def limit(mebibytes):
        return pltpu.CompilerParams(vmem_limit_bytes=mebibytes * 1024 * 1024)

    edges = pl.pallas_call(
        edges_kernel,
        out_shape=(
            shaped(HALO, rows, cols), shaped(HALO, rows, cols),
            shaped(cells_z, HALO, cols), shaped(cells_z, HALO, cols),
            shaped(cells_z, rows, strip),
        ),
        in_specs=[pl.BlockSpec(memory_space=pltpu.HBM)],
        out_specs=(vmem,) * 5,
        scratch_shapes=[pltpu.VMEM((cells_z, RIM, cols), f32)] * 2 + [pltpu.SemaphoreType.DMA((5,))],
        compiler_params=limit(4),
        name="edges",
    )(pltpu.with_memory_space_constraint(block, pltpu.HBM))
    z_first, z_second = pairs(count_z, True)
    y_first, y_second = pairs(count_y, True)
    za = lax.ppermute(edges[0], "gz", z_first)
    zb = lax.ppermute(edges[1], "gz", z_second)
    ya = lax.ppermute(edges[2], "gy", y_first)
    yb = lax.ppermute(edges[3], "gy", y_second)
    edge = lax.ppermute(edges[4], "gx", [(0, 1), (1, 0)])

    image_shape, part_shape = shaped(5, rows, cols), shaped(4, 2, rows, cols)
    image, part, rim = pl.pallas_call(
        functools.partial(inner_kernel, total_z=total_z),
        out_shape=(image_shape, part_shape, shaped(cells_z, 2, 2 * RIM, cols)),
        in_specs=[vmem] * 2,
        out_specs=(vmem,) * 3,
        scratch_shapes=[pltpu.VMEM((rows, cols), f32)] * 4
        + [
            pltpu.VMEM((2 * (cols + strip), cols), jnp.bfloat16),
            pltpu.VMEM((rows, 2 * rows), jnp.bfloat16),
        ],
        compiler_params=limit(16),
        cost_estimate=pl.CostEstimate(
            flops=100 * block.size, bytes_accessed=8 * block.size, transcendentals=6 * block.size
        ),
        name="inner",
    )(block, edge)
    image, part = pl.pallas_call(
        functools.partial(rim_kernel, total_z=total_z, last_y=count_y - 1),
        out_shape=(image_shape, part_shape),
        in_specs=[vmem] * 6,
        out_specs=(vmem,) * 2,
        input_output_aliases={4: 0, 5: 1},
        compiler_params=limit(16),
        cost_estimate=pl.CostEstimate(
            flops=12 * block.size, bytes_accessed=block.size, transcendentals=block.size
        ),
        name="rim",
    )(block, ya, yb, rim, image, part)

    parts = pl.pallas_call(
        functools.partial(outer_kernel, total_z=total_z),
        out_shape=[shaped(5, piece, cols)] * count_z,
        in_specs=[vmem] * 5,
        out_specs=[vmem] * count_z,
        compiler_params=limit(16),
        name="outer",
    )(block, za, zb, image, part)

    out_shape = (shaped(3, piece, cols), shaped(piece, cols), shaped(piece, cols))
    small = limit(8)
    if count_z == 4:
        peers = [
            lax.ppermute(parts[s], "gz", [(i, i ^ s) for i in range(count_z)]) for s in (1, 2, 3)
        ]
        return pl.pallas_call(
            blend_four,
            out_shape=out_shape,
            in_specs=[vmem] * 4,
            out_specs=(vmem, vmem, vmem),
            compiler_params=small,
            name="blend",
        )(parts[0], *peers)
    gathered = lax.all_to_all(jnp.stack(parts), "gz", split_axis=0, concat_axis=0, tiled=True)
    return pl.pallas_call(
        blend_all,
        out_shape=out_shape,
        in_specs=[vmem],
        out_specs=(vmem, vmem, vmem),
        compiler_params=small,
        name="blend",
    )(gathered)


def solution(mesh):
    return jax.shard_map(
        on_device,
        mesh=mesh,
        in_specs=(P("gz", "gy", "gx"),),
        out_specs=(P(None, ("gy", "gz"), "gx"), P(("gy", "gz"), "gx"), P(("gy", "gz"), "gx")),
        check_vma=False,
    )
```

```python
import functools

import jax
import jax.numpy as jnp
from jax import lax
from jax.experimental import pallas as pl
from jax.experimental.pallas import tpu as pltpu
from jax.sharding import PartitionSpec as P

HALO = 2
RIM = 8


def band(offset):
    one = jnp.where(offset == 1, 8.0, jnp.where(offset == -1, -8.0, 0.0))
    two = jnp.where(offset == 2, -1.0, jnp.where(offset == -2, 1.0, 0.0))
    return (one + two).astype(jnp.bfloat16)


def split(value):
    high = value.astype(jnp.bfloat16)
    return high, (value - high.astype(jnp.float32)).astype(jnp.bfloat16)


def dot(a, b):
    return jnp.dot(a, b, preferred_element_type=jnp.float32)


def emit(sample, base, lin, grad_z, depth_step, through, position):
    root = lax.rsqrt(base + grad_z * grad_z * (1.0 / 144.0))
    diffuse = 0.3 + jnp.maximum((lin + grad_z * (0.64 * 0.7 / 12.0)) * root, 0.0)
    grown = jnp.exp(sample)
    optical = jnp.log(1.0 + grown) * ((2.0 - root * root) * depth_step)
    behind = through * jnp.exp(-optical)
    weight = through - behind
    lit = weight * diffuse
    square = grown * grown
    blue = lit / (1.0 + square)
    return behind, (blue * square, lit * jnp.exp(-0.5 * sample * sample), blue, weight * position)


def place():
    return tuple(lax.axis_index(a) for a in ("gx", "gy", "gz"))


def block_of(offset, swapped, at_z):
    return at_z ^ offset if swapped else offset


def edges_kernel(x_ref, *refs, groups, swapped, count_z):
    z_refs, (ya_ref, yb_ref, e_ref, top_ref, bottom_ref, sems) = refs[:-6], refs[-6:]
    cells_z, rows, cols = x_ref.shape
    at_x, at_y, at_z = place()
    strip, piece = e_ref.shape[2], z_refs[0].shape[2]
    even_z, even_y = at_z % 2 == 0, at_y % 2 == 0
    high = cells_z - HALO
    start = pl.multiple_of(jnp.where(at_x == 0, cols - strip, 0), strip)
    after = lax.rem(at_z + 1, count_z)
    before = lax.rem(at_z + count_z - 1, count_z)
    sides = (
        (jnp.where(even_z, after, before), jnp.where(even_z, high, 0)),
        (jnp.where(even_z, before, after), jnp.where(even_z, 0, high)),
    )
    moves = []
    for group, offsets in enumerate(groups):
        for side, (peer, layer) in enumerate(sides):
            for slot, offset in enumerate(offsets):
                row = pl.multiple_of(block_of(offset, swapped, peer) * piece, 8)
                source = x_ref.at[pl.ds(layer, HALO), pl.ds(row, piece)]
                moves.append((source, z_refs[2 * group + side].at[slot]))
    moves += [
        (x_ref.at[:, pl.ds(0, RIM)], top_ref),
        (x_ref.at[:, pl.ds(rows - RIM, RIM)], bottom_ref),
        (x_ref.at[:, :, pl.ds(start, strip)], e_ref),
    ]
    copies = [pltpu.make_async_copy(*move, sems.at[i]) for i, move in enumerate(moves)]
    for copy in copies:
        copy.start()
    for copy in copies:
        copy.wait()
    top, bottom = top_ref[:, :HALO, :], bottom_ref[:, RIM - HALO :, :]
    ya_ref[...] = jnp.where(even_y, bottom, top)
    yb_ref[...] = jnp.where(even_y, top, bottom)


def pair(grad_x, grad_y):
    base = 1.0 + (grad_x * grad_x + grad_y * grad_y) * (1.0 / 144.0)
    lin = grad_x * (0.48 * 0.7 / 12.0) + grad_y * (0.6 * 0.7 / 12.0)
    return base, lin


def inner_kernel(
    x_ref, e_ref, image_ref, part_ref, rim_ref, gx0, gx1, gy0, gy1, wx_ref, wy_ref, *, total_z
):
    cells_z, rows, cols = x_ref.shape
    strip = e_ref.shape[2]
    depth_step = 2.0 / total_z
    at_x, _, at_z = place()
    iota = functools.partial(lax.broadcasted_iota, jnp.int32)
    along_x = band(iota((cols, cols), 0) - iota((cols, cols), 1))
    lane = iota((strip, cols), 0) - iota((strip, cols), 1)
    beyond_x = band(lane + jnp.where(at_x == 0, cols, -strip))
    along_y = band(iota((rows, rows), 1) - iota((rows, rows), 0))
    wx_ref[...] = jnp.concatenate([along_x, along_x, beyond_x, beyond_x], axis=0)
    wy_ref[...] = jnp.concatenate([along_y, along_y], axis=1)

    chunk = 16
    spans = [pl.ds(r, chunk) for r in range(RIM, rows - RIM, chunk)]
    slots = ((gx0, gy0), (gx1, gy1))

    def gradients(k, slot):
        high, low = split(x_ref[k])
        edge_high, edge_low = split(e_ref[k])
        for axis, value in enumerate(
            (
                dot(jnp.concatenate([high, low, edge_high, edge_low], axis=1), wx_ref[...]),
                dot(wy_ref[...], jnp.concatenate([high, low], axis=0)),
            )
        ):
            slots[slot][axis][...] = value
            rim_ref[k, axis, :RIM] = value[:RIM]
            rim_ref[k, axis, RIM:] = value[rows - RIM :]

    def keep(index, slot):
        grad_x, grad_y = slots[slot]
        for at in spans:
            part_ref[index, 0, at], part_ref[index, 1, at] = pair(grad_x[at], grad_y[at])

    def shade(k, slot):
        grad_x, grad_y = slots[slot]
        position = ((at_z * cells_z + k).astype(jnp.float32) + 0.5) / total_z
        for at in spans:
            base, lin = pair(grad_x[at], grad_y[at])
            grad_z = (x_ref[k - 2, at] - x_ref[k + 2, at]) + 8.0 * (x_ref[k + 1, at] - x_ref[k - 1, at])
            through, adds = emit(x_ref[k, at], base, lin, grad_z, depth_step, image_ref[4, at], position)
            image_ref[4, at] = through
            for channel, value in enumerate(adds):
                image_ref[channel, at] += value

    for channel in range(4):
        image_ref[channel] = jnp.zeros((rows, cols), jnp.float32)
    image_ref[4] = jnp.ones((rows, cols), jnp.float32)

    gradients(0, 0)
    gradients(1, 1)
    keep(0, 0)
    gradients(2, 0)
    keep(1, 1)

    @pl.loop(0, (cells_z - 4) // 2)
    def _(step):
        k = 2 + 2 * step
        gradients(k + 1, 1)
        shade(k, 0)
        gradients(k + 2, 0)
        shade(k + 1, 1)

    gradients(cells_z - 1, 1)
    keep(2, 0)
    keep(3, 1)


def rim_kernel(x_ref, ya_ref, yb_ref, rim_ref, image_in, part_in, image_ref, part_ref, *, total_z, last_y):
    del image_in, part_in
    cells_z, rows, cols = x_ref.shape
    depth_step = 2.0 / total_z
    _, at_y, at_z = place()
    even = at_y % 2 == 0
    row = lax.broadcasted_iota(jnp.int32, (RIM, cols), 0)
    zero = jnp.zeros((RIM, cols), jnp.float32)

    def weights(position, there):
        offset = position - row
        one = jnp.where(offset == 1, 8.0, jnp.where(offset == -1, -8.0, 0.0))
        two = jnp.where(offset == 2, -1.0, jnp.where(offset == -2, 1.0, 0.0))
        return jnp.where(there, one + two, zero)

    sides = (
        (0, 0, even, [weights(-HALO + i, at_y > 0) for i in range(HALO)]),
        (RIM, rows - RIM, ~even, [weights(RIM + i, at_y < last_y) for i in range(HALO)]),
    )
    for start, first_row, second, scale in sides:
        at, to = pl.ds(start, RIM), pl.ds(first_row, RIM)

        def planes(k):
            grad_y = rim_ref[k, 1, at]
            for i in range(HALO):
                cell = jnp.where(second, yb_ref[k, i : i + 1], ya_ref[k, i : i + 1])
                grad_y = grad_y + scale[i] * jnp.broadcast_to(cell, (RIM, cols))
            return pair(rim_ref[k, 0, at], grad_y)

        for index, k in enumerate((0, 1, cells_z - 2, cells_z - 1)):
            part_ref[index, 0, to], part_ref[index, 1, to] = planes(k)
        through, sums = zero + 1.0, [zero] * 4
        for k in range(2, cells_z - 2):
            position = ((at_z * cells_z + k).astype(jnp.float32) + 0.5) / total_z
            grad_z = (x_ref[k - 2, to] - x_ref[k + 2, to]) + 8.0 * (x_ref[k + 1, to] - x_ref[k - 1, to])
            base, lin = planes(k)
            through, adds = emit(x_ref[k, to], base, lin, grad_z, depth_step, through, position)
            sums = [s + a for s, a in zip(sums, adds)]
        for channel, value in enumerate(sums + [through]):
            image_ref[channel, to] = value


def outer_kernel(x_ref, za_ref, zb_ref, image_ref, part_ref, *refs, total_z, offsets, swapped):
    cells_z, _, cols = x_ref.shape
    depth_step = 2.0 / total_z
    at_z = place()[2]
    last_z = total_z // cells_z - 1
    even = at_z % 2 == 0
    out_refs = refs[-len(offsets) :]
    piece = out_refs[0].shape[1]
    chunk = min(piece, 16)
    none = jnp.zeros((chunk, cols), jnp.float32)
    for out, start in [(o, s) for o in range(len(offsets)) for s in range(0, piece, chunk)]:
        block = block_of(offsets[out], swapped, at_z)
        part = pl.ds(start, chunk)
        at = pl.ds(pl.multiple_of(block * piece + start, 8), chunk)

        def before(layer):
            return jnp.where(at_z > 0, jnp.where(even, zb_ref[out, layer, part], za_ref[out, layer, part]), none)

        def after(layer):
            return jnp.where(at_z < last_z, jnp.where(even, za_ref[out, layer, part], zb_ref[out, layer, part]), none)

        f = [x_ref[k, at] for k in range(4)]
        b = [x_ref[cells_z - 4 + k, at] for k in range(4)]
        ahead, next_ahead, behind, next_behind = before(0), before(1), after(0), after(1)
        cells = (
            (0, 0, f[0], (ahead - f[2]) + 8.0 * (f[1] - next_ahead)),
            (1, 1, f[1], (next_ahead - f[3]) + 8.0 * (f[2] - f[0])),
            (2, cells_z - 2, b[2], (b[0] - behind) + 8.0 * (b[3] - b[1])),
            (3, cells_z - 1, b[3], (b[1] - next_behind) + 8.0 * (behind - b[2])),
        )
        through = jnp.ones_like(none)
        sums = [none] * 4
        for index, k, sample, grad_z in cells:
            if index == 2:
                sums = [s + through * image_ref[c, at] for c, s in enumerate(sums)]
                through = through * image_ref[4, at]
            position = ((at_z * cells_z + k).astype(jnp.float32) + 0.5) / total_z
            through, adds = emit(
                sample, part_ref[index, 0, at], part_ref[index, 1, at], grad_z, depth_step, through, position
            )
            sums = [s + a for s, a in zip(sums, adds)]
        for channel, value in enumerate(sums + [through]):
            out_refs[out][channel, part] = value


def join(front, back):
    through = front[4]
    return [front[c] + through * back[c] for c in range(4)] + [through * back[4]]


def put(image, colour_ref, depth_ref, clear_ref):
    for channel in range(3):
        colour_ref[channel] = image[channel]
    depth_ref[...] = image[3]
    clear_ref[...] = image[4]


def blend_four(own_ref, one_ref, two_ref, three_ref, colour_ref, depth_ref, clear_ref):
    at_z = place()[2]
    odd, high = at_z % 2 == 1, at_z >= 2
    own, one, two, three = (
        [ref[c] for c in range(5)] for ref in (own_ref, one_ref, two_ref, three_ref)
    )

    def ordered(swap, a, b):
        front = [jnp.where(swap, q, p) for p, q in zip(a, b)]
        back = [jnp.where(swap, p, q) for p, q in zip(a, b)]
        return join(front, back)

    mine = ordered(odd, own, one)
    other = ordered(odd, two, three)
    put(ordered(high, mine, other), colour_ref, depth_ref, clear_ref)


def blend_all(parts_ref, colour_ref, depth_ref, clear_ref):
    image = [parts_ref[0, c] for c in range(5)]
    for k in range(1, parts_ref.shape[0]):
        image = join(image, [parts_ref[k, c] for c in range(5)])
    put(image, colour_ref, depth_ref, clear_ref)


def pairs(count, closed):
    ends = [(0, count - 1), (count - 1, 0)] if closed else [(0, 0), (count - 1, count - 1)]
    first = [(i, i ^ 1) for i in range(count)]
    second = [(i, (i - 1 if i % 2 == 0 else i + 1)) for i in range(1, count - 1)]
    return first, second + ends


def on_device(block):
    cells_z, rows, cols = block.shape
    count_z, count_y = lax.axis_size("gz"), lax.axis_size("gy")
    total_z = cells_z * count_z
    piece = rows // count_z
    strip = 128
    f32 = jnp.float32

    def shaped(*shape):
        return jax.ShapeDtypeStruct(shape, f32)

    vmem = pl.BlockSpec(memory_space=pltpu.VMEM)
    def limit(mebibytes):
        return pltpu.CompilerParams(vmem_limit_bytes=mebibytes * 1024 * 1024)

    swapped = count_z == 4
    groups = ((2, 3), (1, 0)) if swapped else (tuple(range(count_z)),)
    payloads = [shaped(len(g), HALO, piece, cols) for g in groups for _ in range(2)]
    edges = pl.pallas_call(
        functools.partial(edges_kernel, groups=groups, swapped=swapped, count_z=count_z),
        out_shape=payloads
        + [shaped(cells_z, HALO, cols)] * 2
        + [shaped(cells_z, rows, strip)],
        in_specs=[pl.BlockSpec(memory_space=pltpu.HBM)],
        out_specs=[vmem] * (len(payloads) + 3),
        scratch_shapes=[pltpu.VMEM((cells_z, RIM, cols), f32)] * 2
        + [pltpu.SemaphoreType.DMA((2 * sum(len(g) for g in groups) + 3,))],
        compiler_params=limit(4),
        name="edges",
    )(pltpu.with_memory_space_constraint(block, pltpu.HBM))
    z_pairs, (y_first, y_second) = pairs(count_z, True), pairs(count_y, True)
    halos = [
        [lax.ppermute(edges[2 * g + side], "gz", z_pairs[side]) for side in range(2)]
        for g in range(len(groups))
    ]
    ya = lax.ppermute(edges[-3], "gy", y_first)
    yb = lax.ppermute(edges[-2], "gy", y_second)
    edge = lax.ppermute(edges[-1], "gx", [(0, 1), (1, 0)])

    image_shape, part_shape = shaped(5, rows, cols), shaped(4, 2, rows, cols)
    image, part, rim = pl.pallas_call(
        functools.partial(inner_kernel, total_z=total_z),
        out_shape=(image_shape, part_shape, shaped(cells_z, 2, 2 * RIM, cols)),
        in_specs=[vmem] * 2,
        out_specs=(vmem,) * 3,
        scratch_shapes=[pltpu.VMEM((rows, cols), f32)] * 4
        + [
            pltpu.VMEM((2 * (cols + strip), cols), jnp.bfloat16),
            pltpu.VMEM((rows, 2 * rows), jnp.bfloat16),
        ],
        compiler_params=limit(16),
        cost_estimate=pl.CostEstimate(
            flops=100 * block.size, bytes_accessed=8 * block.size, transcendentals=6 * block.size
        ),
        name="inner",
    )(block, edge)
    image, part = pl.pallas_call(
        functools.partial(rim_kernel, total_z=total_z, last_y=count_y - 1),
        out_shape=(image_shape, part_shape),
        in_specs=[vmem] * 6,
        out_specs=(vmem,) * 2,
        input_output_aliases={4: 0, 5: 1},
        compiler_params=limit(16),
        cost_estimate=pl.CostEstimate(
            flops=12 * block.size, bytes_accessed=block.size, transcendentals=block.size
        ),
        name="rim",
    )(block, ya, yb, rim, image, part)

    received = {}
    for offsets, (za, zb) in zip(groups, halos):
        made = pl.pallas_call(
            functools.partial(outer_kernel, total_z=total_z, offsets=offsets, swapped=swapped),
            out_shape=[shaped(5, piece, cols)] * len(offsets),
            in_specs=[vmem] * 5,
            out_specs=[vmem] * len(offsets),
            compiler_params=limit(16),
            name="outer",
        )(block, za, zb, image, part)
        received.update(zip(offsets, made))
    out_shape = (shaped(3, piece, cols), shaped(piece, cols), shaped(piece, cols))
    if swapped:
        for offset in (3, 2, 1):
            swap = [(i, i ^ offset) for i in range(count_z)]
            received[offset] = lax.ppermute(received[offset], "gz", swap)
        return pl.pallas_call(
            blend_four,
            out_shape=out_shape,
            in_specs=[vmem] * 4,
            out_specs=(vmem, vmem, vmem),
            compiler_params=limit(8),
            name="blend",
        )(*(received[offset] for offset in range(4)))
    parts = jnp.stack([received[k] for k in range(count_z)])
    gathered = lax.all_to_all(parts, "gz", split_axis=0, concat_axis=0, tiled=True)
    return pl.pallas_call(
        blend_all,
        out_shape=out_shape,
        in_specs=[vmem],
        out_specs=(vmem, vmem, vmem),
        compiler_params=limit(8),
        name="blend",
    )(gathered)


def solution(mesh):
    return jax.shard_map(
        on_device,
        mesh=mesh,
        in_specs=(P("gz", "gy", "gx"),),
        out_specs=(P(None, ("gy", "gz"), "gx"), P(("gy", "gz"), "gx"), P(("gy", "gz"), "gx")),
        check_vma=False,
    )
```

```python
import functools

import jax
import jax.numpy as jnp
from jax import lax
from jax.experimental import pallas as pl
from jax.experimental.pallas import tpu as pltpu
from jax.sharding import PartitionSpec as P

HALO = 2
RIM = 8


def band(offset):
    one = jnp.where(offset == 1, 8.0, jnp.where(offset == -1, -8.0, 0.0))
    two = jnp.where(offset == 2, -1.0, jnp.where(offset == -2, 1.0, 0.0))
    return (one + two).astype(jnp.bfloat16)


def split(value):
    high = value.astype(jnp.bfloat16)
    return high, (value - high.astype(jnp.float32)).astype(jnp.bfloat16)


def dot(a, b):
    return jnp.dot(a, b, preferred_element_type=jnp.float32)


def emit(sample, base, lin, grad_z, depth_step, through, position):
    root = lax.rsqrt(base + grad_z * grad_z * (1.0 / 144.0))
    diffuse = 0.3 + jnp.maximum((lin + grad_z * (0.64 * 0.7 / 12.0)) * root, 0.0)
    grown = jnp.exp(sample)
    optical = jnp.log(1.0 + grown) * ((2.0 - root * root) * depth_step)
    behind = through * jnp.exp(-optical)
    weight = through - behind
    lit = weight * diffuse
    square = grown * grown
    blue = lit / (1.0 + square)
    return behind, (blue * square, lit * jnp.exp(-0.5 * sample * sample), blue, weight * position)


def place():
    return tuple(lax.axis_index(a) for a in ("gx", "gy", "gz"))


def block_of(offset, swapped, at_z):
    return at_z ^ offset if swapped else offset


def edges_kernel(x_ref, *refs, groups, swapped, count_z):
    z_refs, (ya_ref, yb_ref, e_ref, top_ref, bottom_ref, sems) = refs[:-6], refs[-6:]
    cells_z, rows, cols = x_ref.shape
    at_x, at_y, at_z = place()
    strip, piece = e_ref.shape[2], z_refs[0].shape[2]
    even_z, even_y = at_z % 2 == 0, at_y % 2 == 0
    high = cells_z - HALO
    start = pl.multiple_of(jnp.where(at_x == 0, cols - strip, 0), strip)
    after = lax.rem(at_z + 1, count_z)
    before = lax.rem(at_z + count_z - 1, count_z)
    sides = (
        (jnp.where(even_z, after, before), jnp.where(even_z, high, 0)),
        (jnp.where(even_z, before, after), jnp.where(even_z, 0, high)),
    )
    moves = []
    for group, offsets in enumerate(groups):
        for side, (peer, layer) in enumerate(sides):
            for slot, offset in enumerate(offsets):
                row = pl.multiple_of(block_of(offset, swapped, peer) * piece, 8)
                source = x_ref.at[pl.ds(layer, HALO), pl.ds(row, piece)]
                moves.append((source, z_refs[2 * group + side].at[slot]))
    moves += [
        (x_ref.at[:, pl.ds(0, RIM)], top_ref),
        (x_ref.at[:, pl.ds(rows - RIM, RIM)], bottom_ref),
        (x_ref.at[:, :, pl.ds(start, strip)], e_ref),
    ]
    copies = [pltpu.make_async_copy(*move, sems.at[i]) for i, move in enumerate(moves)]
    for copy in copies:
        copy.start()
    for copy in copies:
        copy.wait()
    top, bottom = top_ref[:, :HALO, :], bottom_ref[:, RIM - HALO :, :]
    ya_ref[...] = jnp.where(even_y, bottom, top)
    yb_ref[...] = jnp.where(even_y, top, bottom)


def pair(grad_x, grad_y):
    base = 1.0 + (grad_x * grad_x + grad_y * grad_y) * (1.0 / 144.0)
    lin = grad_x * (0.48 * 0.7 / 12.0) + grad_y * (0.6 * 0.7 / 12.0)
    return base, lin


def inner_kernel(
    x_ref, e_ref, image_ref, part_ref, rim_ref, gx0, gx1, gy0, gy1, wx_ref, wy_ref, *, total_z
):
    cells_z, rows, cols = x_ref.shape
    strip = e_ref.shape[2]
    depth_step = 2.0 / total_z
    at_x, _, at_z = place()
    iota = functools.partial(lax.broadcasted_iota, jnp.int32)
    along_x = band(iota((cols, cols), 0) - iota((cols, cols), 1))
    lane = iota((strip, cols), 0) - iota((strip, cols), 1)
    beyond_x = band(lane + jnp.where(at_x == 0, cols, -strip))
    along_y = band(iota((rows, rows), 1) - iota((rows, rows), 0))
    wx_ref[...] = jnp.concatenate([along_x, along_x, beyond_x, beyond_x], axis=0)
    wy_ref[...] = jnp.concatenate([along_y, along_y], axis=1)

    chunk = 16
    spans = [pl.ds(r, chunk) for r in range(RIM, rows - RIM, chunk)]
    slots = ((gx0, gy0), (gx1, gy1))

    def gradients(k, slot):
        high, low = split(x_ref[k])
        edge_high, edge_low = split(e_ref[k])
        for axis, value in enumerate(
            (
                dot(jnp.concatenate([high, low, edge_high, edge_low], axis=1), wx_ref[...]),
                dot(wy_ref[...], jnp.concatenate([high, low], axis=0)),
            )
        ):
            slots[slot][axis][...] = value
            rim_ref[k, axis, :RIM] = value[:RIM]
            rim_ref[k, axis, RIM:] = value[rows - RIM :]

    def keep(index, slot):
        grad_x, grad_y = slots[slot]
        for at in spans:
            part_ref[index, 0, at], part_ref[index, 1, at] = pair(grad_x[at], grad_y[at])

    def shade(k, slot):
        grad_x, grad_y = slots[slot]
        position = ((at_z * cells_z + k).astype(jnp.float32) + 0.5) / total_z
        for at in spans:
            base, lin = pair(grad_x[at], grad_y[at])
            grad_z = (x_ref[k - 2, at] - x_ref[k + 2, at]) + 8.0 * (x_ref[k + 1, at] - x_ref[k - 1, at])
            through, adds = emit(x_ref[k, at], base, lin, grad_z, depth_step, image_ref[4, at], position)
            image_ref[4, at] = through
            for channel, value in enumerate(adds):
                image_ref[channel, at] += value

    for channel in range(4):
        image_ref[channel] = jnp.zeros((rows, cols), jnp.float32)
    image_ref[4] = jnp.ones((rows, cols), jnp.float32)

    gradients(0, 0)
    gradients(1, 1)
    keep(0, 0)
    gradients(2, 0)
    keep(1, 1)

    @pl.loop(0, (cells_z - 4) // 2)
    def _(step):
        k = 2 + 2 * step
        gradients(k + 1, 1)
        shade(k, 0)
        gradients(k + 2, 0)
        shade(k + 1, 1)

    gradients(cells_z - 1, 1)
    keep(2, 0)
    keep(3, 1)


def rim_kernel(x_ref, ya_ref, yb_ref, rim_ref, image_in, part_in, image_ref, part_ref, *, total_z, last_y):
    del image_in, part_in
    cells_z, rows, cols = x_ref.shape
    depth_step = 2.0 / total_z
    _, at_y, at_z = place()
    even = at_y % 2 == 0
    row = lax.broadcasted_iota(jnp.int32, (RIM, cols), 0)
    zero = jnp.zeros((RIM, cols), jnp.float32)

    def weights(position, there):
        offset = position - row
        one = jnp.where(offset == 1, 8.0, jnp.where(offset == -1, -8.0, 0.0))
        two = jnp.where(offset == 2, -1.0, jnp.where(offset == -2, 1.0, 0.0))
        return jnp.where(there, one + two, zero)

    sides = (
        (0, 0, even, [weights(-HALO + i, at_y > 0) for i in range(HALO)]),
        (RIM, rows - RIM, ~even, [weights(RIM + i, at_y < last_y) for i in range(HALO)]),
    )
    for start, first_row, second, scale in sides:
        at, to = pl.ds(start, RIM), pl.ds(first_row, RIM)

        def planes(k):
            grad_y = rim_ref[k, 1, at]
            for i in range(HALO):
                cell = jnp.where(second, yb_ref[k, i : i + 1], ya_ref[k, i : i + 1])
                grad_y = grad_y + scale[i] * jnp.broadcast_to(cell, (RIM, cols))
            return pair(rim_ref[k, 0, at], grad_y)

        for index, k in enumerate((0, 1, cells_z - 2, cells_z - 1)):
            part_ref[index, 0, to], part_ref[index, 1, to] = planes(k)
        through, sums = zero + 1.0, [zero] * 4
        for k in range(2, cells_z - 2):
            position = ((at_z * cells_z + k).astype(jnp.float32) + 0.5) / total_z
            grad_z = (x_ref[k - 2, to] - x_ref[k + 2, to]) + 8.0 * (x_ref[k + 1, to] - x_ref[k - 1, to])
            base, lin = planes(k)
            through, adds = emit(x_ref[k, to], base, lin, grad_z, depth_step, through, position)
            sums = [s + a for s, a in zip(sums, adds)]
        for channel, value in enumerate(sums + [through]):
            image_ref[channel, to] = value


def outer_kernel(x_ref, za_ref, zb_ref, image_ref, part_ref, *refs, total_z, offsets, swapped):
    cells_z, _, cols = x_ref.shape
    depth_step = 2.0 / total_z
    at_z = place()[2]
    last_z = total_z // cells_z - 1
    even = at_z % 2 == 0
    out_refs = refs[-len(offsets) :]
    piece = out_refs[0].shape[1]
    chunk = min(piece, 16)
    none = jnp.zeros((chunk, cols), jnp.float32)
    for out, start in [(o, s) for o in range(len(offsets)) for s in range(0, piece, chunk)]:
        block = block_of(offsets[out], swapped, at_z)
        part = pl.ds(start, chunk)
        at = pl.ds(pl.multiple_of(block * piece + start, 8), chunk)

        def before(layer):
            return jnp.where(at_z > 0, jnp.where(even, zb_ref[out, layer, part], za_ref[out, layer, part]), none)

        def after(layer):
            return jnp.where(at_z < last_z, jnp.where(even, za_ref[out, layer, part], zb_ref[out, layer, part]), none)

        f = [x_ref[k, at] for k in range(4)]
        b = [x_ref[cells_z - 4 + k, at] for k in range(4)]
        ahead, next_ahead, behind, next_behind = before(0), before(1), after(0), after(1)
        cells = (
            (0, 0, f[0], (ahead - f[2]) + 8.0 * (f[1] - next_ahead)),
            (1, 1, f[1], (next_ahead - f[3]) + 8.0 * (f[2] - f[0])),
            (2, cells_z - 2, b[2], (b[0] - behind) + 8.0 * (b[3] - b[1])),
            (3, cells_z - 1, b[3], (b[1] - next_behind) + 8.0 * (behind - b[2])),
        )
        through = jnp.ones_like(none)
        sums = [none] * 4
        for index, k, sample, grad_z in cells:
            if index == 2:
                sums = [s + through * image_ref[c, at] for c, s in enumerate(sums)]
                through = through * image_ref[4, at]
            position = ((at_z * cells_z + k).astype(jnp.float32) + 0.5) / total_z
            through, adds = emit(
                sample, part_ref[index, 0, at], part_ref[index, 1, at], grad_z, depth_step, through, position
            )
            sums = [s + a for s, a in zip(sums, adds)]
        for channel, value in enumerate(sums + [through]):
            out_refs[out][channel, part] = value


def join(front, back):
    through = front[4]
    return [front[c] + through * back[c] for c in range(4)] + [through * back[4]]


def put(image, colour_ref, depth_ref, clear_ref):
    for channel in range(3):
        colour_ref[channel] = image[channel]
    depth_ref[...] = image[3]
    clear_ref[...] = image[4]


def blend_four(own_ref, one_ref, two_ref, three_ref, colour_ref, depth_ref, clear_ref):
    at_z = place()[2]
    odd, high = at_z % 2 == 1, at_z >= 2
    own, one, two, three = (
        [ref[c] for c in range(5)] for ref in (own_ref, one_ref, two_ref, three_ref)
    )

    def ordered(swap, a, b):
        front = [jnp.where(swap, q, p) for p, q in zip(a, b)]
        back = [jnp.where(swap, p, q) for p, q in zip(a, b)]
        return join(front, back)

    mine = ordered(odd, own, one)
    other = ordered(odd, two, three)
    put(ordered(high, mine, other), colour_ref, depth_ref, clear_ref)


def blend_all(parts_ref, colour_ref, depth_ref, clear_ref):
    image = [parts_ref[0, c] for c in range(5)]
    for k in range(1, parts_ref.shape[0]):
        image = join(image, [parts_ref[k, c] for c in range(5)])
    put(image, colour_ref, depth_ref, clear_ref)


def pairs(count, closed):
    ends = [(0, count - 1), (count - 1, 0)] if closed else [(0, 0), (count - 1, count - 1)]
    first = [(i, i ^ 1) for i in range(count)]
    second = [(i, (i - 1 if i % 2 == 0 else i + 1)) for i in range(1, count - 1)]
    return first, second + ends


def on_device(block):
    cells_z, rows, cols = block.shape
    count_z, count_y = lax.axis_size("gz"), lax.axis_size("gy")
    total_z = cells_z * count_z
    piece = rows // count_z
    strip = 128
    f32 = jnp.float32

    def shaped(*shape):
        return jax.ShapeDtypeStruct(shape, f32)

    vmem = pl.BlockSpec(memory_space=pltpu.VMEM)
    def limit(mebibytes):
        return pltpu.CompilerParams(vmem_limit_bytes=mebibytes * 1024 * 1024)

    swapped = count_z == 4
    groups = ((2, 3), (1, 0)) if swapped else (tuple(range(count_z)),)
    payloads = [shaped(len(g), HALO, piece, cols) for g in groups for _ in range(2)]
    edges = pl.pallas_call(
        functools.partial(edges_kernel, groups=groups, swapped=swapped, count_z=count_z),
        out_shape=payloads
        + [shaped(cells_z, HALO, cols)] * 2
        + [shaped(cells_z, rows, strip)],
        in_specs=[pl.BlockSpec(memory_space=pltpu.HBM)],
        out_specs=[vmem] * (len(payloads) + 3),
        scratch_shapes=[pltpu.VMEM((cells_z, RIM, cols), f32)] * 2
        + [pltpu.SemaphoreType.DMA((2 * sum(len(g) for g in groups) + 3,))],
        compiler_params=limit(4),
        name="edges",
    )(pltpu.with_memory_space_constraint(block, pltpu.HBM))
    z_pairs, (y_first, y_second) = pairs(count_z, True), pairs(count_y, False)
    halos = [
        [lax.ppermute(edges[2 * g + side], "gz", z_pairs[side]) for side in range(2)]
        for g in range(len(groups))
    ]
    ya = lax.ppermute(edges[-3], "gy", y_first)
    yb = lax.ppermute(edges[-2], "gy", y_second)
    edge = lax.ppermute(edges[-1], "gx", [(0, 1), (1, 0)])

    image_shape, part_shape = shaped(5, rows, cols), shaped(4, 2, rows, cols)
    image, part, rim = pl.pallas_call(
        functools.partial(inner_kernel, total_z=total_z),
        out_shape=(image_shape, part_shape, shaped(cells_z, 2, 2 * RIM, cols)),
        in_specs=[vmem] * 2,
        out_specs=(vmem,) * 3,
        scratch_shapes=[pltpu.VMEM((rows, cols), f32)] * 4
        + [
            pltpu.VMEM((2 * (cols + strip), cols), jnp.bfloat16),
            pltpu.VMEM((rows, 2 * rows), jnp.bfloat16),
        ],
        compiler_params=limit(16),
        cost_estimate=pl.CostEstimate(
            flops=100 * block.size, bytes_accessed=8 * block.size, transcendentals=6 * block.size
        ),
        name="inner",
    )(block, edge)
    image, part = pl.pallas_call(
        functools.partial(rim_kernel, total_z=total_z, last_y=count_y - 1),
        out_shape=(image_shape, part_shape),
        in_specs=[vmem] * 6,
        out_specs=(vmem,) * 2,
        input_output_aliases={4: 0, 5: 1},
        compiler_params=limit(16),
        cost_estimate=pl.CostEstimate(
            flops=12 * block.size, bytes_accessed=block.size, transcendentals=block.size
        ),
        name="rim",
    )(block, ya, yb, rim, image, part)

    received = {}
    for offsets, (za, zb) in zip(groups, halos):
        made = pl.pallas_call(
            functools.partial(outer_kernel, total_z=total_z, offsets=offsets, swapped=swapped),
            out_shape=[shaped(5, piece, cols)] * len(offsets),
            in_specs=[vmem] * 5,
            out_specs=[vmem] * len(offsets),
            compiler_params=limit(16),
            name="outer",
        )(block, za, zb, image, part)
        received.update(zip(offsets, made))
    out_shape = (shaped(3, piece, cols), shaped(piece, cols), shaped(piece, cols))
    if swapped:
        for offset in (3, 2, 1):
            swap = [(i, i ^ offset) for i in range(count_z)]
            received[offset] = lax.ppermute(received[offset], "gz", swap)
        return pl.pallas_call(
            blend_four,
            out_shape=out_shape,
            in_specs=[vmem] * 4,
            out_specs=(vmem, vmem, vmem),
            compiler_params=limit(8),
            name="blend",
        )(*(received[offset] for offset in range(4)))
    parts = jnp.stack([received[k] for k in range(count_z)])
    gathered = lax.all_to_all(parts, "gz", split_axis=0, concat_axis=0, tiled=True)
    return pl.pallas_call(
        blend_all,
        out_shape=out_shape,
        in_specs=[vmem],
        out_specs=(vmem, vmem, vmem),
        compiler_params=limit(8),
        name="blend",
    )(gathered)


def solution(mesh):
    return jax.shard_map(
        on_device,
        mesh=mesh,
        in_specs=(P("gz", "gy", "gx"),),
        out_specs=(P(None, ("gy", "gz"), "gx"), P(("gy", "gz"), "gx"), P(("gy", "gz"), "gx")),
        check_vma=False,
    )
```

```python
import functools

import jax
import jax.numpy as jnp
from jax import lax
from jax.experimental import pallas as pl
from jax.experimental.pallas import tpu as pltpu
from jax.sharding import PartitionSpec as P

HALO = 2
RIM = 8


def band(offset):
    one = jnp.where(offset == 1, 8.0, jnp.where(offset == -1, -8.0, 0.0))
    two = jnp.where(offset == 2, -1.0, jnp.where(offset == -2, 1.0, 0.0))
    return (one + two).astype(jnp.bfloat16)


def split(value):
    high = value.astype(jnp.bfloat16)
    return high, (value - high.astype(jnp.float32)).astype(jnp.bfloat16)


def dot(a, b):
    return jnp.dot(a, b, preferred_element_type=jnp.float32)


def emit(sample, base, lin, grad_z, depth_step, through, position):
    root = lax.rsqrt(base + grad_z * grad_z * (1.0 / 144.0))
    diffuse = 0.3 + jnp.maximum((lin + grad_z * (0.64 * 0.7 / 12.0)) * root, 0.0)
    grown = jnp.exp(sample)
    optical = jnp.log(1.0 + grown) * ((2.0 - root * root) * depth_step)
    behind = through * jnp.exp(-optical)
    weight = through - behind
    lit = weight * diffuse
    square = grown * grown
    blue = lit / (1.0 + square)
    return behind, (blue * square, lit * jnp.exp(-0.5 * sample * sample), blue, weight * position)


def place():
    return tuple(lax.axis_index(a) for a in ("gx", "gy", "gz"))


def block_of(offset, swapped, at_z):
    return at_z ^ offset if swapped else offset


def edges_kernel(x_ref, *refs, sends, swapped, count_z):
    z_refs, (ya_ref, yb_ref, e_ref, top_ref, bottom_ref, sems) = refs[:-6], refs[-6:]
    cells_z, rows, cols = x_ref.shape
    at_x, at_y, at_z = place()
    strip, piece = e_ref.shape[2], z_refs[0].shape[2]
    even_z, even_y = at_z % 2 == 0, at_y % 2 == 0
    high = cells_z - HALO
    start = pl.multiple_of(jnp.where(at_x == 0, cols - strip, 0), strip)
    after = lax.rem(at_z + 1, count_z)
    before = lax.rem(at_z + count_z - 1, count_z)
    sides = (
        (jnp.where(even_z, after, before), jnp.where(even_z, high, 0)),
        (jnp.where(even_z, before, after), jnp.where(even_z, 0, high)),
    )
    moves = []
    for z_ref, (side, offsets) in zip(z_refs, sends):
        peer, layer = sides[side]
        for slot, offset in enumerate(offsets):
            row = pl.multiple_of(block_of(offset, swapped, peer) * piece, 8)
            moves.append((x_ref.at[pl.ds(layer, HALO), pl.ds(row, piece)], z_ref.at[slot]))
    moves += [
        (x_ref.at[:, pl.ds(0, RIM)], top_ref),
        (x_ref.at[:, pl.ds(rows - RIM, RIM)], bottom_ref),
        (x_ref.at[:, :, pl.ds(start, strip)], e_ref),
    ]
    copies = [pltpu.make_async_copy(*move, sems.at[i]) for i, move in enumerate(moves)]
    for copy in copies:
        copy.start()
    for copy in copies:
        copy.wait()
    top, bottom = top_ref[:, :HALO, :], bottom_ref[:, RIM - HALO :, :]
    ya_ref[...] = jnp.where(even_y, bottom, top)
    yb_ref[...] = jnp.where(even_y, top, bottom)


def pair(grad_x, grad_y):
    base = 1.0 + (grad_x * grad_x + grad_y * grad_y) * (1.0 / 144.0)
    lin = grad_x * (0.48 * 0.7 / 12.0) + grad_y * (0.6 * 0.7 / 12.0)
    return base, lin


def inner_kernel(
    x_ref, e_ref, image_ref, part_ref, rim_ref, gx0, gx1, gy0, gy1, wx_ref, wy_ref, *, total_z
):
    cells_z, rows, cols = x_ref.shape
    strip = e_ref.shape[2]
    depth_step = 2.0 / total_z
    at_x, _, at_z = place()
    iota = functools.partial(lax.broadcasted_iota, jnp.int32)
    along_x = band(iota((cols, cols), 0) - iota((cols, cols), 1))
    lane = iota((strip, cols), 0) - iota((strip, cols), 1)
    beyond_x = band(lane + jnp.where(at_x == 0, cols, -strip))
    along_y = band(iota((rows, rows), 1) - iota((rows, rows), 0))
    wx_ref[...] = jnp.concatenate([along_x, along_x, beyond_x, beyond_x], axis=0)
    wy_ref[...] = jnp.concatenate([along_y, along_y], axis=1)

    chunk = 16
    spans = [pl.ds(r, chunk) for r in range(RIM, rows - RIM, chunk)]
    slots = ((gx0, gy0), (gx1, gy1))

    def gradients(k, slot):
        high, low = split(x_ref[k])
        edge_high, edge_low = split(e_ref[k])
        for axis, value in enumerate(
            (
                dot(jnp.concatenate([high, low, edge_high, edge_low], axis=1), wx_ref[...]),
                dot(wy_ref[...], jnp.concatenate([high, low], axis=0)),
            )
        ):
            slots[slot][axis][...] = value
            rim_ref[k, axis, :RIM] = value[:RIM]
            rim_ref[k, axis, RIM:] = value[rows - RIM :]

    def keep(index, slot):
        grad_x, grad_y = slots[slot]
        for at in spans:
            part_ref[index, 0, at], part_ref[index, 1, at] = pair(grad_x[at], grad_y[at])

    def shade(k, slot):
        grad_x, grad_y = slots[slot]
        position = ((at_z * cells_z + k).astype(jnp.float32) + 0.5) / total_z
        for at in spans:
            base, lin = pair(grad_x[at], grad_y[at])
            grad_z = (x_ref[k - 2, at] - x_ref[k + 2, at]) + 8.0 * (x_ref[k + 1, at] - x_ref[k - 1, at])
            through, adds = emit(x_ref[k, at], base, lin, grad_z, depth_step, image_ref[4, at], position)
            image_ref[4, at] = through
            for channel, value in enumerate(adds):
                image_ref[channel, at] += value

    for channel in range(4):
        image_ref[channel] = jnp.zeros((rows, cols), jnp.float32)
    image_ref[4] = jnp.ones((rows, cols), jnp.float32)

    gradients(0, 0)
    gradients(1, 1)
    keep(0, 0)
    gradients(2, 0)
    keep(1, 1)

    @pl.loop(0, (cells_z - 4) // 2)
    def _(step):
        k = 2 + 2 * step
        gradients(k + 1, 1)
        shade(k, 0)
        gradients(k + 2, 0)
        shade(k + 1, 1)

    gradients(cells_z - 1, 1)
    keep(2, 0)
    keep(3, 1)


def rim_kernel(x_ref, ya_ref, yb_ref, rim_ref, image_in, part_in, image_ref, part_ref, *, total_z, last_y):
    del image_in, part_in
    cells_z, rows, cols = x_ref.shape
    depth_step = 2.0 / total_z
    _, at_y, at_z = place()
    even = at_y % 2 == 0
    row = lax.broadcasted_iota(jnp.int32, (RIM, cols), 0)
    zero = jnp.zeros((RIM, cols), jnp.float32)

    def weights(position, there):
        offset = position - row
        one = jnp.where(offset == 1, 8.0, jnp.where(offset == -1, -8.0, 0.0))
        two = jnp.where(offset == 2, -1.0, jnp.where(offset == -2, 1.0, 0.0))
        return jnp.where(there, one + two, zero)

    sides = (
        (0, 0, even, [weights(-HALO + i, at_y > 0) for i in range(HALO)]),
        (RIM, rows - RIM, ~even, [weights(RIM + i, at_y < last_y) for i in range(HALO)]),
    )
    for start, first_row, second, scale in sides:
        at, to = pl.ds(start, RIM), pl.ds(first_row, RIM)

        def planes(k):
            grad_y = rim_ref[k, 1, at]
            for i in range(HALO):
                cell = jnp.where(second, yb_ref[k, i : i + 1], ya_ref[k, i : i + 1])
                grad_y = grad_y + scale[i] * jnp.broadcast_to(cell, (RIM, cols))
            return pair(rim_ref[k, 0, at], grad_y)

        for index, k in enumerate((0, 1, cells_z - 2, cells_z - 1)):
            part_ref[index, 0, to], part_ref[index, 1, to] = planes(k)
        through, sums = zero + 1.0, [zero] * 4
        for k in range(2, cells_z - 2):
            position = ((at_z * cells_z + k).astype(jnp.float32) + 0.5) / total_z
            grad_z = (x_ref[k - 2, to] - x_ref[k + 2, to]) + 8.0 * (x_ref[k + 1, to] - x_ref[k - 1, to])
            base, lin = planes(k)
            through, adds = emit(x_ref[k, to], base, lin, grad_z, depth_step, through, position)
            sums = [s + a for s, a in zip(sums, adds)]
        for channel, value in enumerate(sums + [through]):
            image_ref[channel, to] = value


def outer_kernel(x_ref, za_ref, zb_ref, image_ref, part_ref, *refs, total_z, offsets, swapped, base):
    cells_z, _, cols = x_ref.shape
    depth_step = 2.0 / total_z
    at_z = place()[2]
    last_z = total_z // cells_z - 1
    even = at_z % 2 == 0
    out_refs = refs[-len(offsets) :]
    piece = out_refs[0].shape[1]
    chunk = min(piece, 16)
    none = jnp.zeros((chunk, cols), jnp.float32)
    for out, start in [(o, s) for o in range(len(offsets)) for s in range(0, piece, chunk)]:
        block = block_of(offsets[out], swapped, at_z)
        part = pl.ds(start, chunk)
        at = pl.ds(pl.multiple_of(block * piece + start, 8), chunk)

        def before(layer):
            return jnp.where(at_z > 0, jnp.where(even, zb_ref[out, layer, part], za_ref[base + out, layer, part]), none)

        def after(layer):
            return jnp.where(at_z < last_z, jnp.where(even, za_ref[base + out, layer, part], zb_ref[out, layer, part]), none)

        f = [x_ref[k, at] for k in range(4)]
        b = [x_ref[cells_z - 4 + k, at] for k in range(4)]
        ahead, next_ahead, behind, next_behind = before(0), before(1), after(0), after(1)
        cells = (
            (0, 0, f[0], (ahead - f[2]) + 8.0 * (f[1] - next_ahead)),
            (1, 1, f[1], (next_ahead - f[3]) + 8.0 * (f[2] - f[0])),
            (2, cells_z - 2, b[2], (b[0] - behind) + 8.0 * (b[3] - b[1])),
            (3, cells_z - 1, b[3], (b[1] - next_behind) + 8.0 * (behind - b[2])),
        )
        through = jnp.ones_like(none)
        sums = [none] * 4
        for index, k, sample, grad_z in cells:
            if index == 2:
                sums = [s + through * image_ref[c, at] for c, s in enumerate(sums)]
                through = through * image_ref[4, at]
            position = ((at_z * cells_z + k).astype(jnp.float32) + 0.5) / total_z
            through, adds = emit(
                sample, part_ref[index, 0, at], part_ref[index, 1, at], grad_z, depth_step, through, position
            )
            sums = [s + a for s, a in zip(sums, adds)]
        for channel, value in enumerate(sums + [through]):
            out_refs[out][channel, part] = value


def join(front, back):
    through = front[4]
    return [front[c] + through * back[c] for c in range(4)] + [through * back[4]]


def put(image, colour_ref, depth_ref, clear_ref):
    for channel in range(3):
        colour_ref[channel] = image[channel]
    depth_ref[...] = image[3]
    clear_ref[...] = image[4]


def blend_four(own_ref, one_ref, two_ref, three_ref, colour_ref, depth_ref, clear_ref):
    at_z = place()[2]
    odd, high = at_z % 2 == 1, at_z >= 2
    own, one, two, three = (
        [ref[c] for c in range(5)] for ref in (own_ref, one_ref, two_ref, three_ref)
    )

    def ordered(swap, a, b):
        front = [jnp.where(swap, q, p) for p, q in zip(a, b)]
        back = [jnp.where(swap, p, q) for p, q in zip(a, b)]
        return join(front, back)

    mine = ordered(odd, own, one)
    other = ordered(odd, two, three)
    put(ordered(high, mine, other), colour_ref, depth_ref, clear_ref)


def blend_all(parts_ref, colour_ref, depth_ref, clear_ref):
    image = [parts_ref[0, c] for c in range(5)]
    for k in range(1, parts_ref.shape[0]):
        image = join(image, [parts_ref[k, c] for c in range(5)])
    put(image, colour_ref, depth_ref, clear_ref)


def swap_pairs(value, axis, second):
    count = lax.axis_size(axis)
    if not second:
        return lax.ppermute(value, axis, [(i, i ^ 1) for i in range(count)])
    pairs = []
    for core in range(2):
        for i in range(count):
            peer = i - 1 if i % 2 == 0 else i + 1
            inside = 0 <= peer < count
            to = core * count + peer if inside else (1 - core) * count + i
            pairs.append((core * count + i, to))
    return lax.ppermute(value, ("gx", axis), pairs)


def on_device(block):
    cells_z, rows, cols = block.shape
    count_z, count_y = lax.axis_size("gz"), lax.axis_size("gy")
    total_z = cells_z * count_z
    piece = rows // count_z
    strip = 128
    f32 = jnp.float32

    def shaped(*shape):
        return jax.ShapeDtypeStruct(shape, f32)

    vmem = pl.BlockSpec(memory_space=pltpu.VMEM)
    def limit(mebibytes):
        return pltpu.CompilerParams(vmem_limit_bytes=mebibytes * 1024 * 1024)

    swapped = count_z == 4
    groups = ((2, 3), (1, 0)) if swapped else (tuple(range(count_z)),)
    every = sum(groups, ())
    sends = [(0, every)] + [(1, g) for g in groups]
    payloads = [shaped(len(g), HALO, piece, cols) for _, g in sends]
    edges = pl.pallas_call(
        functools.partial(edges_kernel, sends=sends, swapped=swapped, count_z=count_z),
        out_shape=payloads
        + [shaped(cells_z, HALO, cols)] * 2
        + [shaped(cells_z, rows, strip)],
        in_specs=[pl.BlockSpec(memory_space=pltpu.HBM)],
        out_specs=[vmem] * (len(payloads) + 3),
        scratch_shapes=[pltpu.VMEM((cells_z, RIM, cols), f32)] * 2
        + [pltpu.SemaphoreType.DMA((2 * len(every) + 3,))],
        compiler_params=limit(4),
        name="edges",
    )(pltpu.with_memory_space_constraint(block, pltpu.HBM))
    whole, *cut = [
        swap_pairs(value, "gz", side) for value, (side, _) in zip(edges, sends)
    ]
    ya = swap_pairs(edges[-3], "gy", False)
    yb = swap_pairs(edges[-2], "gy", True)
    edge = lax.ppermute(edges[-1], "gx", [(0, 1), (1, 0)])

    image_shape, part_shape = shaped(5, rows, cols), shaped(4, 2, rows, cols)
    image, part, rim = pl.pallas_call(
        functools.partial(inner_kernel, total_z=total_z),
        out_shape=(image_shape, part_shape, shaped(cells_z, 2, 2 * RIM, cols)),
        in_specs=[vmem] * 2,
        out_specs=(vmem,) * 3,
        scratch_shapes=[pltpu.VMEM((rows, cols), f32)] * 4
        + [
            pltpu.VMEM((2 * (cols + strip), cols), jnp.bfloat16),
            pltpu.VMEM((rows, 2 * rows), jnp.bfloat16),
        ],
        compiler_params=limit(16),
        cost_estimate=pl.CostEstimate(
            flops=100 * block.size, bytes_accessed=8 * block.size, transcendentals=6 * block.size
        ),
        name="inner",
    )(block, edge)
    image, part = pl.pallas_call(
        functools.partial(rim_kernel, total_z=total_z, last_y=count_y - 1),
        out_shape=(image_shape, part_shape),
        in_specs=[vmem] * 6,
        out_specs=(vmem,) * 2,
        input_output_aliases={4: 0, 5: 1},
        compiler_params=limit(16),
        cost_estimate=pl.CostEstimate(
            flops=12 * block.size, bytes_accessed=block.size, transcendentals=block.size
        ),
        name="rim",
    )(block, ya, yb, rim, image, part)

    received = {}
    for offsets, own in zip(groups, cut):
        za, zb = whole, own
        made = pl.pallas_call(
            functools.partial(outer_kernel, total_z=total_z, offsets=offsets, swapped=swapped, base=every.index(offsets[0])),
            out_shape=[shaped(5, piece, cols)] * len(offsets),
            in_specs=[vmem] * 5,
            out_specs=[vmem] * len(offsets),
            compiler_params=limit(16),
            name="outer",
        )(block, za, zb, image, part)
        received.update(zip(offsets, made))
    out_shape = (shaped(3, piece, cols), shaped(piece, cols), shaped(piece, cols))
    if swapped:
        for offset in (3, 2, 1):
            swap = [(i, i ^ offset) for i in range(count_z)]
            received[offset] = lax.ppermute(received[offset], "gz", swap)
        return pl.pallas_call(
            blend_four,
            out_shape=out_shape,
            in_specs=[vmem] * 4,
            out_specs=(vmem, vmem, vmem),
            compiler_params=limit(8),
            name="blend",
        )(*(received[offset] for offset in range(4)))
    parts = jnp.stack([received[k] for k in range(count_z)])
    gathered = lax.all_to_all(parts, "gz", split_axis=0, concat_axis=0, tiled=True)
    return pl.pallas_call(
        blend_all,
        out_shape=out_shape,
        in_specs=[vmem],
        out_specs=(vmem, vmem, vmem),
        compiler_params=limit(8),
        name="blend",
    )(gathered)


def solution(mesh):
    return jax.shard_map(
        on_device,
        mesh=mesh,
        in_specs=(P("gz", "gy", "gx"),),
        out_specs=(P(None, ("gy", "gz"), "gx"), P(("gy", "gz"), "gx"), P(("gy", "gz"), "gx")),
        check_vma=False,
    )
```

```python
import functools

import jax
import jax.numpy as jnp
from jax import lax
from jax.experimental import pallas as pl
from jax.experimental.pallas import tpu as pltpu
from jax.sharding import PartitionSpec as P

HALO = 2
RIM = 8


def band(offset):
    one = jnp.where(offset == 1, 8.0, jnp.where(offset == -1, -8.0, 0.0))
    two = jnp.where(offset == 2, -1.0, jnp.where(offset == -2, 1.0, 0.0))
    return (one + two).astype(jnp.bfloat16)


def split(value):
    high = value.astype(jnp.bfloat16)
    return high, (value - high.astype(jnp.float32)).astype(jnp.bfloat16)


def dot(a, b):
    return jnp.dot(a, b, preferred_element_type=jnp.float32)


def emit(sample, base, lin, grad_z, depth_step, through, position):
    root = lax.rsqrt(base + grad_z * grad_z * (1.0 / 144.0))
    diffuse = 0.3 + jnp.maximum((lin + grad_z * (0.64 * 0.7 / 12.0)) * root, 0.0)
    grown = jnp.exp(sample)
    optical = jnp.log(1.0 + grown) * ((2.0 - root * root) * depth_step)
    behind = through * jnp.exp(-optical)
    weight = through - behind
    lit = weight * diffuse
    square = grown * grown
    blue = lit / (1.0 + square)
    return behind, (blue * square, lit * jnp.exp(-0.5 * sample * sample), blue, weight * position)


def place():
    return tuple(lax.axis_index(a) for a in ("gx", "gy", "gz"))


def block_of(offset, swapped, at_z):
    return at_z ^ offset if swapped else offset


def depth_moves(x_ref, z_refs, sends, swapped, count_z):
    piece = z_refs[0].shape[2]
    at_z = place()[2]
    even = at_z % 2 == 0
    high = x_ref.shape[0] - HALO
    after = lax.rem(at_z + 1, count_z)
    before = lax.rem(at_z + count_z - 1, count_z)
    sides = (
        (jnp.where(even, after, before), jnp.where(even, high, 0)),
        (jnp.where(even, before, after), jnp.where(even, 0, high)),
    )
    moves = []
    for z_ref, (side, offsets) in zip(z_refs, sends):
        peer, layer = sides[side]
        for slot, offset in enumerate(offsets):
            row = pl.multiple_of(block_of(offset, swapped, peer) * piece, 8)
            moves.append((x_ref.at[pl.ds(layer, HALO), pl.ds(row, piece)], z_ref.at[slot]))
    return moves


def copy_all(moves, sems):
    copies = [pltpu.make_async_copy(*move, sems.at[i]) for i, move in enumerate(moves)]
    for copy in copies:
        copy.start()
    for copy in copies:
        copy.wait()


def edges_kernel(x_ref, *refs, sends, swapped, count_z):
    z_refs, (ya_ref, yb_ref, e_ref, top_ref, bottom_ref, sems) = refs[:-6], refs[-6:]
    _, rows, cols = x_ref.shape
    at_x, at_y, _ = place()
    strip = e_ref.shape[2]
    even = at_y % 2 == 0
    start = pl.multiple_of(jnp.where(at_x == 0, cols - strip, 0), strip)
    moves = depth_moves(x_ref, z_refs, sends, swapped, count_z)
    moves += [
        (x_ref.at[:, pl.ds(0, RIM)], top_ref),
        (x_ref.at[:, pl.ds(rows - RIM, RIM)], bottom_ref),
        (x_ref.at[:, :, pl.ds(start, strip)], e_ref),
    ]
    copy_all(moves, sems)
    top, bottom = top_ref[:, :HALO, :], bottom_ref[:, RIM - HALO :, :]
    ya_ref[...] = jnp.where(even, bottom, top)
    yb_ref[...] = jnp.where(even, top, bottom)


def late_edges_kernel(x_ref, *refs, sends, swapped, count_z):
    z_refs = refs[-1 - len(sends) : -1]
    copy_all(depth_moves(x_ref, z_refs, sends, swapped, count_z), refs[-1])


def pair(grad_x, grad_y):
    base = 1.0 + (grad_x * grad_x + grad_y * grad_y) * (1.0 / 144.0)
    lin = grad_x * (0.48 * 0.7 / 12.0) + grad_y * (0.6 * 0.7 / 12.0)
    return base, lin


def inner_kernel(
    x_ref, e_ref, image_ref, part_ref, rim_ref, gx0, gx1, gy0, gy1, wx_ref, wy_ref, *, total_z
):
    cells_z, rows, cols = x_ref.shape
    strip = e_ref.shape[2]
    depth_step = 2.0 / total_z
    at_x, _, at_z = place()
    iota = functools.partial(lax.broadcasted_iota, jnp.int32)
    along_x = band(iota((cols, cols), 0) - iota((cols, cols), 1))
    lane = iota((strip, cols), 0) - iota((strip, cols), 1)
    beyond_x = band(lane + jnp.where(at_x == 0, cols, -strip))
    along_y = band(iota((rows, rows), 1) - iota((rows, rows), 0))
    wx_ref[...] = jnp.concatenate([along_x, along_x, beyond_x, beyond_x], axis=0)
    wy_ref[...] = jnp.concatenate([along_y, along_y], axis=1)

    chunk = 16
    spans = [pl.ds(r, chunk) for r in range(RIM, rows - RIM, chunk)]
    slots = ((gx0, gy0), (gx1, gy1))

    def gradients(k, slot):
        high, low = split(x_ref[k])
        edge_high, edge_low = split(e_ref[k])
        for axis, value in enumerate(
            (
                dot(jnp.concatenate([high, low, edge_high, edge_low], axis=1), wx_ref[...]),
                dot(wy_ref[...], jnp.concatenate([high, low], axis=0)),
            )
        ):
            slots[slot][axis][...] = value
            rim_ref[k, axis, :RIM] = value[:RIM]
            rim_ref[k, axis, RIM:] = value[rows - RIM :]

    def keep(index, slot):
        grad_x, grad_y = slots[slot]
        for at in spans:
            part_ref[index, 0, at], part_ref[index, 1, at] = pair(grad_x[at], grad_y[at])

    def shade(k, slot):
        grad_x, grad_y = slots[slot]
        position = ((at_z * cells_z + k).astype(jnp.float32) + 0.5) / total_z
        for at in spans:
            base, lin = pair(grad_x[at], grad_y[at])
            grad_z = (x_ref[k - 2, at] - x_ref[k + 2, at]) + 8.0 * (x_ref[k + 1, at] - x_ref[k - 1, at])
            through, adds = emit(x_ref[k, at], base, lin, grad_z, depth_step, image_ref[4, at], position)
            image_ref[4, at] = through
            for channel, value in enumerate(adds):
                image_ref[channel, at] += value

    for channel in range(4):
        image_ref[channel] = jnp.zeros((rows, cols), jnp.float32)
    image_ref[4] = jnp.ones((rows, cols), jnp.float32)

    gradients(0, 0)
    gradients(1, 1)
    keep(0, 0)
    gradients(2, 0)
    keep(1, 1)

    @pl.loop(0, (cells_z - 4) // 2)
    def _(step):
        k = 2 + 2 * step
        gradients(k + 1, 1)
        shade(k, 0)
        gradients(k + 2, 0)
        shade(k + 1, 1)

    gradients(cells_z - 1, 1)
    keep(2, 0)
    keep(3, 1)


def rim_kernel(x_ref, ya_ref, yb_ref, rim_ref, image_in, part_in, image_ref, part_ref, *, total_z, last_y):
    del image_in, part_in
    cells_z, rows, cols = x_ref.shape
    depth_step = 2.0 / total_z
    _, at_y, at_z = place()
    even = at_y % 2 == 0
    row = lax.broadcasted_iota(jnp.int32, (RIM, cols), 0)
    zero = jnp.zeros((RIM, cols), jnp.float32)

    def weights(position, there):
        offset = position - row
        one = jnp.where(offset == 1, 8.0, jnp.where(offset == -1, -8.0, 0.0))
        two = jnp.where(offset == 2, -1.0, jnp.where(offset == -2, 1.0, 0.0))
        return jnp.where(there, one + two, zero)

    sides = (
        (0, 0, even, [weights(-HALO + i, at_y > 0) for i in range(HALO)]),
        (RIM, rows - RIM, ~even, [weights(RIM + i, at_y < last_y) for i in range(HALO)]),
    )
    for start, first_row, second, scale in sides:
        at, to = pl.ds(start, RIM), pl.ds(first_row, RIM)

        def planes(k):
            grad_y = rim_ref[k, 1, at]
            for i in range(HALO):
                cell = jnp.where(second, yb_ref[k, i : i + 1], ya_ref[k, i : i + 1])
                grad_y = grad_y + scale[i] * jnp.broadcast_to(cell, (RIM, cols))
            return pair(rim_ref[k, 0, at], grad_y)

        for index, k in enumerate((0, 1, cells_z - 2, cells_z - 1)):
            part_ref[index, 0, to], part_ref[index, 1, to] = planes(k)
        through, sums = zero + 1.0, [zero] * 4
        for k in range(2, cells_z - 2):
            position = ((at_z * cells_z + k).astype(jnp.float32) + 0.5) / total_z
            grad_z = (x_ref[k - 2, to] - x_ref[k + 2, to]) + 8.0 * (x_ref[k + 1, to] - x_ref[k - 1, to])
            base, lin = planes(k)
            through, adds = emit(x_ref[k, to], base, lin, grad_z, depth_step, through, position)
            sums = [s + a for s, a in zip(sums, adds)]
        for channel, value in enumerate(sums + [through]):
            image_ref[channel, to] = value


def outer_kernel(x_ref, za_ref, zb_ref, image_ref, part_ref, *refs, total_z, offsets, swapped, base, zb_base):
    cells_z, _, cols = x_ref.shape
    depth_step = 2.0 / total_z
    at_z = place()[2]
    last_z = total_z // cells_z - 1
    even = at_z % 2 == 0
    out_refs = refs[-len(offsets) :]
    piece = out_refs[0].shape[1]
    chunk = min(piece, 16)
    none = jnp.zeros((chunk, cols), jnp.float32)
    for out, start in [(o, s) for o in range(len(offsets)) for s in range(0, piece, chunk)]:
        block = block_of(offsets[out], swapped, at_z)
        part = pl.ds(start, chunk)
        at = pl.ds(pl.multiple_of(block * piece + start, 8), chunk)

        def before(layer):
            return jnp.where(at_z > 0, jnp.where(even, zb_ref[zb_base + out, layer, part], za_ref[base + out, layer, part]), none)

        def after(layer):
            return jnp.where(at_z < last_z, jnp.where(even, za_ref[base + out, layer, part], zb_ref[zb_base + out, layer, part]), none)

        f = [x_ref[k, at] for k in range(4)]
        b = [x_ref[cells_z - 4 + k, at] for k in range(4)]
        ahead, next_ahead, behind, next_behind = before(0), before(1), after(0), after(1)
        cells = (
            (0, 0, f[0], (ahead - f[2]) + 8.0 * (f[1] - next_ahead)),
            (1, 1, f[1], (next_ahead - f[3]) + 8.0 * (f[2] - f[0])),
            (2, cells_z - 2, b[2], (b[0] - behind) + 8.0 * (b[3] - b[1])),
            (3, cells_z - 1, b[3], (b[1] - next_behind) + 8.0 * (behind - b[2])),
        )
        through = jnp.ones_like(none)
        sums = [none] * 4
        for index, k, sample, grad_z in cells:
            if index == 2:
                sums = [s + through * image_ref[c, at] for c, s in enumerate(sums)]
                through = through * image_ref[4, at]
            position = ((at_z * cells_z + k).astype(jnp.float32) + 0.5) / total_z
            through, adds = emit(
                sample, part_ref[index, 0, at], part_ref[index, 1, at], grad_z, depth_step, through, position
            )
            sums = [s + a for s, a in zip(sums, adds)]
        for channel, value in enumerate(sums + [through]):
            out_refs[out][channel, part] = value


def join(front, back):
    through = front[4]
    return [front[c] + through * back[c] for c in range(4)] + [through * back[4]]


def put(image, colour_ref, depth_ref, clear_ref):
    for channel in range(3):
        colour_ref[channel] = image[channel]
    depth_ref[...] = image[3]
    clear_ref[...] = image[4]


def blend_four(own_ref, one_ref, three_ref, two_ref, colour_ref, depth_ref, clear_ref):
    at_z = place()[2]
    odd, high = at_z % 2 == 1, at_z >= 2
    own, one, two, three = (
        [ref[c] for c in range(5)] for ref in (own_ref, one_ref, two_ref, three_ref)
    )

    def ordered(swap, a, b):
        front = [jnp.where(swap, q, p) for p, q in zip(a, b)]
        back = [jnp.where(swap, p, q) for p, q in zip(a, b)]
        return join(front, back)

    mine = ordered(odd, own, one)
    other = ordered(odd, two, three)
    put(ordered(high, mine, other), colour_ref, depth_ref, clear_ref)


def blend_all(parts_ref, colour_ref, depth_ref, clear_ref):
    image = [parts_ref[0, c] for c in range(5)]
    for k in range(1, parts_ref.shape[0]):
        image = join(image, [parts_ref[k, c] for c in range(5)])
    put(image, colour_ref, depth_ref, clear_ref)


def swap_pairs(value, axis, second):
    count = lax.axis_size(axis)
    if not second:
        return lax.ppermute(value, axis, [(i, i ^ 1) for i in range(count)])
    pairs = []
    for core in range(2):
        for i in range(count):
            peer = i - 1 if i % 2 == 0 else i + 1
            inside = 0 <= peer < count
            to = core * count + peer if inside else (1 - core) * count + i
            pairs.append((core * count + i, to))
    return lax.ppermute(value, ("gx", axis), pairs)


def on_device(block):
    cells_z, rows, cols = block.shape
    count_z, count_y = lax.axis_size("gz"), lax.axis_size("gy")
    total_z = cells_z * count_z
    piece = rows // count_z
    strip = 128
    f32 = jnp.float32

    def shaped(*shape):
        return jax.ShapeDtypeStruct(shape, f32)

    vmem = pl.BlockSpec(memory_space=pltpu.VMEM)
    def limit(mebibytes):
        return pltpu.CompilerParams(vmem_limit_bytes=mebibytes * 1024 * 1024)

    swapped = count_z == 4
    groups = ((2, 3), (1, 0)) if swapped else (tuple(range(count_z)),)
    every = sum(groups, ())
    sends = [(0, every)] + [(1, g) for g in groups]
    early, late = sends[:2], sends[2:]
    payloads = [shaped(len(g), HALO, piece, cols) for _, g in sends]
    edges = pl.pallas_call(
        functools.partial(edges_kernel, sends=early, swapped=swapped, count_z=count_z),
        out_shape=payloads[:2]
        + [shaped(cells_z, HALO, cols)] * 2
        + [shaped(cells_z, rows, strip)],
        in_specs=[pl.BlockSpec(memory_space=pltpu.HBM)],
        out_specs=[vmem] * 5,
        scratch_shapes=[pltpu.VMEM((cells_z, RIM, cols), f32)] * 2
        + [pltpu.SemaphoreType.DMA((sum(len(g) for _, g in early) + 3,))],
        compiler_params=limit(4),
        name="edges",
    )(pltpu.with_memory_space_constraint(block, pltpu.HBM))
    halos = [swap_pairs(value, "gz", side) for value, (side, _) in zip(edges, early)]
    ya = swap_pairs(edges[-3], "gy", False)
    yb = swap_pairs(edges[-2], "gy", True)
    edge = lax.ppermute(edges[-1], "gx", [(0, 1), (1, 0)])

    image_shape, part_shape = shaped(5, rows, cols), shaped(4, 2, rows, cols)
    image, part, rim = pl.pallas_call(
        functools.partial(inner_kernel, total_z=total_z),
        out_shape=(image_shape, part_shape, shaped(cells_z, 2, 2 * RIM, cols)),
        in_specs=[vmem] * 2,
        out_specs=(vmem,) * 3,
        scratch_shapes=[pltpu.VMEM((rows, cols), f32)] * 4
        + [
            pltpu.VMEM((2 * (cols + strip), cols), jnp.bfloat16),
            pltpu.VMEM((rows, 2 * rows), jnp.bfloat16),
        ],
        compiler_params=limit(16),
        cost_estimate=pl.CostEstimate(
            flops=100 * block.size, bytes_accessed=8 * block.size, transcendentals=6 * block.size
        ),
        name="inner",
    )(block, edge)
    if late:
        last = pl.pallas_call(
            functools.partial(late_edges_kernel, sends=late, swapped=swapped, count_z=count_z),
            out_shape=payloads[2:],
            in_specs=[vmem] + [pl.BlockSpec(memory_space=pl.ANY)] * 3,
            out_specs=[vmem] * len(late),
            scratch_shapes=[pltpu.SemaphoreType.DMA((sum(len(g) for _, g in late),))],
            compiler_params=limit(4),
            name="late_edges",
        )(block, rim, ya, yb)
        halos += [swap_pairs(value, "gz", side) for value, (side, _) in zip(last, late)]
    whole, *cut = halos
    image, part = pl.pallas_call(
        functools.partial(rim_kernel, total_z=total_z, last_y=count_y - 1),
        out_shape=(image_shape, part_shape),
        in_specs=[vmem] * 6,
        out_specs=(vmem,) * 2,
        input_output_aliases={4: 0, 5: 1},
        compiler_params=limit(16),
        cost_estimate=pl.CostEstimate(
            flops=12 * block.size, bytes_accessed=block.size, transcendentals=block.size
        ),
        name="rim",
    )(block, ya, yb, rim, image, part)

    received = {}
    for offsets in [(o,) for o in every] if swapped else groups:
        base = every.index(offsets[0])
        zb, zb_base = next((c, g.index(offsets[0])) for c, g in zip(cut, groups) if offsets[0] in g)
        made = pl.pallas_call(
            functools.partial(
                outer_kernel, total_z=total_z, offsets=offsets, swapped=swapped, base=base, zb_base=zb_base
            ),
            out_shape=[shaped(5, piece, cols)] * len(offsets),
            in_specs=[vmem] * 5,
            out_specs=[vmem] * len(offsets),
            compiler_params=limit(16),
            name="outer",
        )(block, whole, zb, image, part)
        received.update(zip(offsets, made))
    out_shape = (shaped(3, piece, cols), shaped(piece, cols), shaped(piece, cols))
    if swapped:
        for offset in (3, 2, 1):
            swap = [(i, i ^ offset) for i in range(count_z)]
            received[offset] = lax.ppermute(received[offset], "gz", swap)
        return pl.pallas_call(
            blend_four,
            out_shape=out_shape,
            in_specs=[vmem] * 4,
            out_specs=(vmem, vmem, vmem),
            compiler_params=limit(8),
            name="blend",
        )(*(received[offset] for offset in (0, 1, 3, 2)))
    parts = jnp.stack([received[k] for k in range(count_z)])
    gathered = lax.all_to_all(parts, "gz", split_axis=0, concat_axis=0, tiled=True)
    return pl.pallas_call(
        blend_all,
        out_shape=out_shape,
        in_specs=[vmem],
        out_specs=(vmem, vmem, vmem),
        compiler_params=limit(8),
        name="blend",
    )(gathered)


def solution(mesh):
    return jax.shard_map(
        on_device,
        mesh=mesh,
        in_specs=(P("gz", "gy", "gx"),),
        out_specs=(P(None, ("gy", "gz"), "gx"), P(("gy", "gz"), "gx"), P(("gy", "gz"), "gx")),
        check_vma=False,
    )
```

```python
import functools

import jax
import jax.numpy as jnp
from jax import lax
from jax.experimental import pallas as pl
from jax.experimental.pallas import tpu as pltpu
from jax.sharding import PartitionSpec as P

HALO = 2
RIM = 8


def band(offset):
    one = jnp.where(offset == 1, 8.0, jnp.where(offset == -1, -8.0, 0.0))
    two = jnp.where(offset == 2, -1.0, jnp.where(offset == -2, 1.0, 0.0))
    return (one + two).astype(jnp.bfloat16)


def split(value):
    high = value.astype(jnp.bfloat16)
    return high, (value - high.astype(jnp.float32)).astype(jnp.bfloat16)


def dot(a, b):
    return jnp.dot(a, b, preferred_element_type=jnp.float32)


def emit(sample, base, lin, grad_z, depth_step, through, position):
    root = lax.rsqrt(base + grad_z * grad_z * (1.0 / 144.0))
    diffuse = 0.3 + jnp.maximum((lin + grad_z * (0.64 * 0.7 / 12.0)) * root, 0.0)
    grown = jnp.exp(sample)
    optical = jnp.log(1.0 + grown) * ((2.0 - root * root) * depth_step)
    behind = through * jnp.exp(-optical)
    weight = through - behind
    lit = weight * diffuse
    square = grown * grown
    blue = lit / (1.0 + square)
    return behind, (blue * square, lit * jnp.exp(-0.5 * sample * sample), blue, weight * position)


def place():
    return tuple(lax.axis_index(a) for a in ("gx", "gy", "gz"))


def block_of(offset, swapped, at_z):
    return at_z ^ offset if swapped else offset


def depth_moves(x_ref, z_refs, sends, swapped, count_z):
    piece = z_refs[0].shape[2]
    at_z = place()[2]
    even = at_z % 2 == 0
    high = x_ref.shape[0] - HALO
    after = lax.rem(at_z + 1, count_z)
    before = lax.rem(at_z + count_z - 1, count_z)
    sides = (
        (jnp.where(even, after, before), jnp.where(even, high, 0)),
        (jnp.where(even, before, after), jnp.where(even, 0, high)),
    )
    moves = []
    for z_ref, (side, offsets) in zip(z_refs, sends):
        peer, layer = sides[side]
        for slot, offset in enumerate(offsets):
            row = pl.multiple_of(block_of(offset, swapped, peer) * piece, 8)
            moves.append((x_ref.at[pl.ds(layer, HALO), pl.ds(row, piece)], z_ref.at[slot]))
    return moves


def copy_all(moves, sems):
    copies = [pltpu.make_async_copy(*move, sems.at[i]) for i, move in enumerate(moves)]
    for copy in copies:
        copy.start()
    for copy in copies:
        copy.wait()


def edges_kernel(x_ref, *refs, sends, swapped, count_z):
    z_refs, (ya_ref, yb_ref, e_ref, top_ref, bottom_ref, sems) = refs[:-6], refs[-6:]
    _, rows, cols = x_ref.shape
    at_x, at_y, _ = place()
    strip = e_ref.shape[2]
    even = at_y % 2 == 0
    start = pl.multiple_of(jnp.where(at_x == 0, cols - strip, 0), strip)
    moves = depth_moves(x_ref, z_refs, sends, swapped, count_z)
    moves += [
        (x_ref.at[:, pl.ds(0, RIM)], top_ref),
        (x_ref.at[:, pl.ds(rows - RIM, RIM)], bottom_ref),
        (x_ref.at[:, :, pl.ds(start, strip)], e_ref),
    ]
    copy_all(moves, sems)
    top, bottom = top_ref[:, :HALO, :], bottom_ref[:, RIM - HALO :, :]
    ya_ref[...] = jnp.where(even, bottom, top)
    yb_ref[...] = jnp.where(even, top, bottom)


def late_edges_kernel(x_ref, *refs, sends, swapped, count_z):
    z_refs = refs[-1 - len(sends) : -1]
    copy_all(depth_moves(x_ref, z_refs, sends, swapped, count_z), refs[-1])


def pair(grad_x, grad_y):
    base = 1.0 + (grad_x * grad_x + grad_y * grad_y) * (1.0 / 144.0)
    lin = grad_x * (0.48 * 0.7 / 12.0) + grad_y * (0.6 * 0.7 / 12.0)
    return base, lin


def inner_kernel(
    x_ref, e_ref, image_ref, part_ref, rim_ref, gx0, gx1, gy0, gy1, wx_ref, wy_ref, *, total_z
):
    cells_z, rows, cols = x_ref.shape
    strip = e_ref.shape[2]
    depth_step = 2.0 / total_z
    at_x, _, at_z = place()
    iota = functools.partial(lax.broadcasted_iota, jnp.int32)
    along_x = band(iota((cols, cols), 0) - iota((cols, cols), 1))
    lane = iota((strip, cols), 0) - iota((strip, cols), 1)
    beyond_x = band(lane + jnp.where(at_x == 0, cols, -strip))
    along_y = band(iota((rows, rows), 1) - iota((rows, rows), 0))
    wx_ref[...] = jnp.concatenate([along_x, along_x, beyond_x, beyond_x], axis=0)
    wy_ref[...] = jnp.concatenate([along_y, along_y], axis=1)

    chunk = 8
    spans = [pl.ds(r, chunk) for r in range(RIM, rows - RIM, chunk)]
    slots = ((gx0, gy0), (gx1, gy1))

    def gradients(k, slot):
        high, low = split(x_ref[k])
        edge_high, edge_low = split(e_ref[k])
        for axis, value in enumerate(
            (
                dot(jnp.concatenate([high, low, edge_high, edge_low], axis=1), wx_ref[...]),
                dot(wy_ref[...], jnp.concatenate([high, low], axis=0)),
            )
        ):
            slots[slot][axis][...] = value
            rim_ref[k, axis, :RIM] = value[:RIM]
            rim_ref[k, axis, RIM:] = value[rows - RIM :]

    def keep(index, slot):
        grad_x, grad_y = slots[slot]
        for at in spans:
            part_ref[index, 0, at], part_ref[index, 1, at] = pair(grad_x[at], grad_y[at])

    def shade(k, slot):
        grad_x, grad_y = slots[slot]
        position = ((at_z * cells_z + k).astype(jnp.float32) + 0.5) / total_z
        for at in spans:
            base, lin = pair(grad_x[at], grad_y[at])
            grad_z = (x_ref[k - 2, at] - x_ref[k + 2, at]) + 8.0 * (x_ref[k + 1, at] - x_ref[k - 1, at])
            through, adds = emit(x_ref[k, at], base, lin, grad_z, depth_step, image_ref[4, at], position)
            image_ref[4, at] = through
            for channel, value in enumerate(adds):
                image_ref[channel, at] += value

    for channel in range(4):
        image_ref[channel] = jnp.zeros((rows, cols), jnp.float32)
    image_ref[4] = jnp.ones((rows, cols), jnp.float32)

    gradients(0, 0)
    gradients(1, 1)
    keep(0, 0)
    gradients(2, 0)
    keep(1, 1)

    @pl.loop(0, (cells_z - 4) // 2)
    def _(step):
        k = 2 + 2 * step
        gradients(k + 1, 1)
        shade(k, 0)
        gradients(k + 2, 0)
        shade(k + 1, 1)

    gradients(cells_z - 1, 1)
    keep(2, 0)
    keep(3, 1)


def rim_kernel(x_ref, ya_ref, yb_ref, rim_ref, image_in, part_in, image_ref, part_ref, *, total_z, last_y):
    del image_in, part_in
    cells_z, rows, cols = x_ref.shape
    depth_step = 2.0 / total_z
    _, at_y, at_z = place()
    even = at_y % 2 == 0
    row = lax.broadcasted_iota(jnp.int32, (RIM, cols), 0)
    zero = jnp.zeros((RIM, cols), jnp.float32)

    def weights(position, there):
        offset = position - row
        one = jnp.where(offset == 1, 8.0, jnp.where(offset == -1, -8.0, 0.0))
        two = jnp.where(offset == 2, -1.0, jnp.where(offset == -2, 1.0, 0.0))
        return jnp.where(there, one + two, zero)

    sides = (
        (0, 0, even, [weights(-HALO + i, at_y > 0) for i in range(HALO)]),
        (RIM, rows - RIM, ~even, [weights(RIM + i, at_y < last_y) for i in range(HALO)]),
    )
    for start, first_row, second, scale in sides:
        at, to = pl.ds(start, RIM), pl.ds(first_row, RIM)

        def planes(k):
            grad_y = rim_ref[k, 1, at]
            for i in range(HALO):
                cell = jnp.where(second, yb_ref[k, i : i + 1], ya_ref[k, i : i + 1])
                grad_y = grad_y + scale[i] * jnp.broadcast_to(cell, (RIM, cols))
            return pair(rim_ref[k, 0, at], grad_y)

        for index, k in enumerate((0, 1, cells_z - 2, cells_z - 1)):
            part_ref[index, 0, to], part_ref[index, 1, to] = planes(k)
        through, sums = zero + 1.0, [zero] * 4
        for k in range(2, cells_z - 2):
            position = ((at_z * cells_z + k).astype(jnp.float32) + 0.5) / total_z
            grad_z = (x_ref[k - 2, to] - x_ref[k + 2, to]) + 8.0 * (x_ref[k + 1, to] - x_ref[k - 1, to])
            base, lin = planes(k)
            through, adds = emit(x_ref[k, to], base, lin, grad_z, depth_step, through, position)
            sums = [s + a for s, a in zip(sums, adds)]
        for channel, value in enumerate(sums + [through]):
            image_ref[channel, to] = value


def outer_kernel(x_ref, za_ref, zb_ref, image_ref, part_ref, *refs, total_z, offsets, swapped, base, zb_base):
    cells_z, _, cols = x_ref.shape
    depth_step = 2.0 / total_z
    at_z = place()[2]
    last_z = total_z // cells_z - 1
    even = at_z % 2 == 0
    out_refs = refs[-len(offsets) :]
    piece = out_refs[0].shape[1]
    chunk = min(piece, 16)
    none = jnp.zeros((chunk, cols), jnp.float32)
    for out, start in [(o, s) for o in range(len(offsets)) for s in range(0, piece, chunk)]:
        block = block_of(offsets[out], swapped, at_z)
        part = pl.ds(start, chunk)
        at = pl.ds(pl.multiple_of(block * piece + start, 8), chunk)

        def before(layer):
            return jnp.where(at_z > 0, jnp.where(even, zb_ref[zb_base + out, layer, part], za_ref[base + out, layer, part]), none)

        def after(layer):
            return jnp.where(at_z < last_z, jnp.where(even, za_ref[base + out, layer, part], zb_ref[zb_base + out, layer, part]), none)

        f = [x_ref[k, at] for k in range(4)]
        b = [x_ref[cells_z - 4 + k, at] for k in range(4)]
        ahead, next_ahead, behind, next_behind = before(0), before(1), after(0), after(1)
        cells = (
            (0, 0, f[0], (ahead - f[2]) + 8.0 * (f[1] - next_ahead)),
            (1, 1, f[1], (next_ahead - f[3]) + 8.0 * (f[2] - f[0])),
            (2, cells_z - 2, b[2], (b[0] - behind) + 8.0 * (b[3] - b[1])),
            (3, cells_z - 1, b[3], (b[1] - next_behind) + 8.0 * (behind - b[2])),
        )
        through = jnp.ones_like(none)
        sums = [none] * 4
        for index, k, sample, grad_z in cells:
            if index == 2:
                sums = [s + through * image_ref[c, at] for c, s in enumerate(sums)]
                through = through * image_ref[4, at]
            position = ((at_z * cells_z + k).astype(jnp.float32) + 0.5) / total_z
            through, adds = emit(
                sample, part_ref[index, 0, at], part_ref[index, 1, at], grad_z, depth_step, through, position
            )
            sums = [s + a for s, a in zip(sums, adds)]
        for channel, value in enumerate(sums + [through]):
            out_refs[out][channel, part] = value


def join(front, back):
    through = front[4]
    return [front[c] + through * back[c] for c in range(4)] + [through * back[4]]


def put(image, colour_ref, depth_ref, clear_ref):
    for channel in range(3):
        colour_ref[channel] = image[channel]
    depth_ref[...] = image[3]
    clear_ref[...] = image[4]


def blend_four(own_ref, one_ref, three_ref, two_ref, colour_ref, depth_ref, clear_ref):
    at_z = place()[2]
    odd, high = at_z % 2 == 1, at_z >= 2
    own, one, two, three = (
        [ref[c] for c in range(5)] for ref in (own_ref, one_ref, two_ref, three_ref)
    )

    def ordered(swap, a, b):
        front = [jnp.where(swap, q, p) for p, q in zip(a, b)]
        back = [jnp.where(swap, p, q) for p, q in zip(a, b)]
        return join(front, back)

    mine = ordered(odd, own, one)
    other = ordered(odd, two, three)
    put(ordered(high, mine, other), colour_ref, depth_ref, clear_ref)


def blend_all(parts_ref, colour_ref, depth_ref, clear_ref):
    image = [parts_ref[0, c] for c in range(5)]
    for k in range(1, parts_ref.shape[0]):
        image = join(image, [parts_ref[k, c] for c in range(5)])
    put(image, colour_ref, depth_ref, clear_ref)


def swap_pairs(value, axis, second):
    count = lax.axis_size(axis)
    if not second:
        return lax.ppermute(value, axis, [(i, i ^ 1) for i in range(count)])
    pairs = []
    for core in range(2):
        for i in range(count):
            peer = i - 1 if i % 2 == 0 else i + 1
            inside = 0 <= peer < count
            to = core * count + peer if inside else (1 - core) * count + i
            pairs.append((core * count + i, to))
    return lax.ppermute(value, ("gx", axis), pairs)


def on_device(block):
    cells_z, rows, cols = block.shape
    count_z, count_y = lax.axis_size("gz"), lax.axis_size("gy")
    total_z = cells_z * count_z
    piece = rows // count_z
    strip = 128
    f32 = jnp.float32

    def shaped(*shape):
        return jax.ShapeDtypeStruct(shape, f32)

    vmem = pl.BlockSpec(memory_space=pltpu.VMEM)
    def limit(mebibytes):
        return pltpu.CompilerParams(vmem_limit_bytes=mebibytes * 1024 * 1024)

    swapped = count_z == 4
    groups = ((2, 3), (1, 0)) if swapped else (tuple(range(count_z)),)
    every = sum(groups, ())
    sends = [(0, every)] + [(1, g) for g in groups]
    early, late = sends[:2], sends[2:]
    payloads = [shaped(len(g), HALO, piece, cols) for _, g in sends]
    edges = pl.pallas_call(
        functools.partial(edges_kernel, sends=early, swapped=swapped, count_z=count_z),
        out_shape=payloads[:2]
        + [shaped(cells_z, HALO, cols)] * 2
        + [shaped(cells_z, rows, strip)],
        in_specs=[pl.BlockSpec(memory_space=pltpu.HBM)],
        out_specs=[vmem] * 5,
        scratch_shapes=[pltpu.VMEM((cells_z, RIM, cols), f32)] * 2
        + [pltpu.SemaphoreType.DMA((sum(len(g) for _, g in early) + 3,))],
        compiler_params=limit(4),
        name="edges",
    )(pltpu.with_memory_space_constraint(block, pltpu.HBM))
    halos = [swap_pairs(value, "gz", side) for value, (side, _) in zip(edges, early)]
    ya = swap_pairs(edges[-3], "gy", False)
    yb = swap_pairs(edges[-2], "gy", True)
    edge = lax.ppermute(edges[-1], "gx", [(0, 1), (1, 0)])

    image_shape, part_shape = shaped(5, rows, cols), shaped(4, 2, rows, cols)
    image, part, rim = pl.pallas_call(
        functools.partial(inner_kernel, total_z=total_z),
        out_shape=(image_shape, part_shape, shaped(cells_z, 2, 2 * RIM, cols)),
        in_specs=[vmem] * 2,
        out_specs=(vmem,) * 3,
        scratch_shapes=[pltpu.VMEM((rows, cols), f32)] * 4
        + [
            pltpu.VMEM((2 * (cols + strip), cols), jnp.bfloat16),
            pltpu.VMEM((rows, 2 * rows), jnp.bfloat16),
        ],
        compiler_params=limit(16),
        cost_estimate=pl.CostEstimate(
            flops=100 * block.size, bytes_accessed=8 * block.size, transcendentals=6 * block.size
        ),
        name="inner",
    )(block, edge)
    if late:
        last = pl.pallas_call(
            functools.partial(late_edges_kernel, sends=late, swapped=swapped, count_z=count_z),
            out_shape=payloads[2:],
            in_specs=[vmem] + [pl.BlockSpec(memory_space=pl.ANY)] * 3,
            out_specs=[vmem] * len(late),
            scratch_shapes=[pltpu.SemaphoreType.DMA((sum(len(g) for _, g in late),))],
            compiler_params=limit(4),
            name="late_edges",
        )(block, rim, ya, yb)
        halos += [swap_pairs(value, "gz", side) for value, (side, _) in zip(last, late)]
    whole, *cut = halos
    image, part = pl.pallas_call(
        functools.partial(rim_kernel, total_z=total_z, last_y=count_y - 1),
        out_shape=(image_shape, part_shape),
        in_specs=[vmem] * 6,
        out_specs=(vmem,) * 2,
        input_output_aliases={4: 0, 5: 1},
        compiler_params=limit(16),
        cost_estimate=pl.CostEstimate(
            flops=12 * block.size, bytes_accessed=block.size, transcendentals=block.size
        ),
        name="rim",
    )(block, ya, yb, rim, image, part)

    received = {}
    for offsets in [(o,) for o in every] if swapped else groups:
        base = every.index(offsets[0])
        zb, zb_base = next((c, g.index(offsets[0])) for c, g in zip(cut, groups) if offsets[0] in g)
        made = pl.pallas_call(
            functools.partial(
                outer_kernel, total_z=total_z, offsets=offsets, swapped=swapped, base=base, zb_base=zb_base
            ),
            out_shape=[shaped(5, piece, cols)] * len(offsets),
            in_specs=[vmem] * 5,
            out_specs=[vmem] * len(offsets),
            compiler_params=limit(16),
            name="outer",
        )(block, whole, zb, image, part)
        received.update(zip(offsets, made))
    out_shape = (shaped(3, piece, cols), shaped(piece, cols), shaped(piece, cols))
    if swapped:
        for offset in (3, 2, 1):
            swap = [(i, i ^ offset) for i in range(count_z)]
            received[offset] = lax.ppermute(received[offset], "gz", swap)
        return pl.pallas_call(
            blend_four,
            out_shape=out_shape,
            in_specs=[vmem] * 4,
            out_specs=(vmem, vmem, vmem),
            compiler_params=limit(8),
            name="blend",
        )(*(received[offset] for offset in (0, 1, 3, 2)))
    parts = jnp.stack([received[k] for k in range(count_z)])
    gathered = lax.all_to_all(parts, "gz", split_axis=0, concat_axis=0, tiled=True)
    return pl.pallas_call(
        blend_all,
        out_shape=out_shape,
        in_specs=[vmem],
        out_specs=(vmem, vmem, vmem),
        compiler_params=limit(8),
        name="blend",
    )(gathered)


def solution(mesh):
    return jax.shard_map(
        on_device,
        mesh=mesh,
        in_specs=(P("gz", "gy", "gx"),),
        out_specs=(P(None, ("gy", "gz"), "gx"), P(("gy", "gz"), "gx"), P(("gy", "gz"), "gx")),
        check_vma=False,
    )
```
